32 devices in a mesh: ens: 2 (over y), tm: 4 (over x, core), lat: 4 (over z).
Axes of the slice: x: 2, y: 2, z: 4, core: 2. Of those that a mesh axis runs over, the one named last changes fastest.
Arguments:
- departures: float32 [8, 8, 69, 256], P(('ens', 'tm'), 'lat'), parts along dimension 0, may hold values from -6 to 6
- error_precision: float32 [8, 8, 69, 256], P(('ens', 'tm'), 'lat'), parts along dimension 0, may hold values from 0.5 to 4
- trajectory: bfloat16 [8, 8, 69, 256], P(('ens', 'tm'), 'lat'), parts along dimension 0, may hold values from -6 to 6
- conv_in: bfloat16 [3, 3, 128, 69], replicated, may hold values from -0.25 to 0.25
- conv_out: bfloat16 [3, 3, 69, 128], replicated, may hold values from -0.1875 to 0.1875
- hidden_bias: float32 [128], replicated, may hold values from -1 to 1
- step_counts: int32 [8], P(('ens', 'tm')), parts along dimension 0, may hold values from 1 to 2, as said below
- obs_tiles: int32 [8, 1024], P(('ens', 'tm'), 'lat'), parts along dimension 0, may hold values from 0 to 275
- obs_weights: float32 [8, 1024, 128], P(('ens', 'tm'), 'lat'), parts along dimension 0, may hold values from -0.5 to 0.5
- innovations: float32 [8, 1024], P(('ens', 'tm'), 'lat'), parts along dimension 0, may hold values from -6 to 6
- obs_precision: float32 [8, 1024], P(('ens', 'tm'), 'lat'), parts along dimension 0, may hold values from 0.5 to 4
Outputs:
- increment: float32 [8, 8, 69, 256], P(('ens', 'tm'), 'lat'), parts along dimension 0
- residual: float32 [8, 8, 69, 256], P(('ens', 'tm'), 'lat'), parts along dimension 0
The draws below stay inside these ranges and needn't reach their ends.
There are 2 independent parts, one for each index of `ens`. The reference program is written for one: setup_inputs(seed, part) draws one part's arguments, and reference() takes and returns one part's arrays. A program takes and returns all parts, laid end to end along the dimension named above; an argument that names none is the same for every part. Nothing has to cross between parts.
Inputs may be any that keep to these rules, and one draw needn't show every extreme that they name: sub-window k runs step_counts[k] of its 2 hourly steps; some sub-window runs all of them.
All inputs are finite; a program needn't handle non-finite values.
Results may differ from the reference program's by a relative error of at most 0.02.
Values may be sent and summed in bfloat16 or wider, within the bound.
No kernel may reach another device: no remote copies, remote signals or barrier semaphores. Data moves between devices by JAX's collectives and lax.ppermute only.
A program may use at most 64 MiB of HBM per device.

```python
import math
import jax
import jax.numpy as jnp

C = 69
HID = 128
TILE = 128
STEPS = 2
ITERS = 2
LON = 256
OBS_DEV = 256
SUBWIN = 4
NROWS = 8
OBSERV = 1024
TILES = 276
N_LAT = 4


def draw_step_counts(key, part):
    draw_key, pick_key = jax.random.split(jax.random.fold_in(key, 17))
    counts = jax.random.randint(draw_key, (SUBWIN,), 1, STEPS + 1)
    chosen = jax.random.randint(pick_key, (), 0, SUBWIN)
    return jnp.where(jnp.arange(SUBWIN) == chosen, STEPS, counts).astype(jnp.int32)


def plant(drawn, key, least, largest):
    index_at = [jax.random.randint(jax.random.fold_in(key, axis), (), 0, length) for axis, length in enumerate(drawn.shape)]
    longest = drawn.shape.index(max(drawn.shape))
    beside = index_at[:longest] + [(index_at[longest] + 1) % drawn.shape[longest]] + index_at[longest + 1:]
    return drawn.at[tuple(index_at)].set(least).at[tuple(beside)].set(largest)


def levels(key, extent, pieces, least, high):
    loudness = 1.0
    for dim, blocks in pieces:
        steps = jax.random.uniform(jax.random.fold_in(jax.random.fold_in(key, 6), dim), (blocks,), jnp.float32, least / len(pieces), high / len(pieces))
        loudness = loudness * jnp.repeat(jnp.exp(steps), extent[dim] // blocks).reshape((-1,) + (1,) * (len(extent) - 1 - dim))
    return loudness


def normal_values(own_key, shape, scale, most, shards=(), held_as=jnp.bfloat16):
    entries = jax.random.normal(own_key, shape, jnp.float32) * scale
    if len(shards) > 0:
        entries = levels(own_key, shape, shards, -0.22, 0.18) * entries
    return jnp.clip(entries, min=-most, max=most).astype(held_as)


def setup_inputs(seed: int = 0, part: int = 0) -> dict:
    streams_of = jax.random.split(jax.random.key(seed), 12)
    own_keys = jax.random.split(jax.random.fold_in(streams_of[11], part), 12)
    return {
        "departures": normal_values(own_keys[0], (SUBWIN, NROWS, C, LON), 1.0, 6.0, ((0, 4), (1, 4)), jnp.float32),
        "error_precision": jnp.clip(jnp.exp(math.log(4.0) - 2.0794415 * jax.random.uniform(own_keys[1], (SUBWIN, NROWS, C, LON), jnp.float32) ** levels(own_keys[1], (SUBWIN, NROWS, C, LON), ((0, 4), (1, 4)), -0.2, 0.2)), 0.5, 4.0),
        "trajectory": normal_values(own_keys[2], (SUBWIN, NROWS, C, LON), 1.0, 6.0, ((0, 4), (1, 4))),
        "conv_in": normal_values(streams_of[3], (3, 3, HID, C), (9 * C) ** -0.5, 0.25),
        "conv_out": normal_values(streams_of[4], (3, 3, C, HID), (9 * HID) ** -0.5, 0.1875),
        "hidden_bias": jnp.clip(jax.random.uniform(streams_of[5], (HID,), jnp.float32, -1.0, 1.0), -1.0, 1.0),
        "step_counts": draw_step_counts(jax.random.fold_in(jax.random.fold_in(streams_of[11], part), 71), part),
        "obs_tiles": plant(jax.random.randint(own_keys[7], (SUBWIN, OBSERV), 0, TILES), jax.random.fold_in(own_keys[7], 1), 0, TILES - 1).astype(jnp.int32),
        "obs_weights": normal_values(own_keys[8], (SUBWIN, OBSERV, TILE), TILE ** -0.5, 0.5, ((0, 4), (1, 4)), jnp.float32),
        "innovations": normal_values(own_keys[9], (SUBWIN, OBSERV), 1.0, 6.0, ((0, 4), (1, 4)), jnp.float32),
        "obs_precision": jnp.clip(jnp.exp(math.log(4.0) - 2.0794415 * jax.random.uniform(own_keys[10], (SUBWIN, OBSERV), jnp.float32) ** levels(own_keys[10], (SUBWIN, OBSERV), ((0, 4), (1, 4)), -0.2, 0.2)), 0.5, 4.0),
    }


def convolve(source, kernel):
    out_rows = source.shape[-3]
    lon_len = source.shape[-1]
    pad_spec = [(0, 0)] * (source.ndim - 3) + [(1, 1), (0, 0), (0, 0)]
    padded = jnp.pad(source, pad_spec)
    wrapped = jnp.concatenate([padded[..., -1:], padded, padded[..., :1]], axis=-1)
    accumulated = None
    for row_off in range(3):
        for col_off in range(3):
            window = wrapped[..., row_off:row_off + out_rows, :, col_off:col_off + lon_len]
            term = jnp.einsum("oi,...ril->...rol", kernel[row_off, col_off].astype(jnp.float32), window.astype(jnp.float32))
            accumulated = term if accumulated is None else accumulated + term
    return accumulated


def flipped(kernel):
    return jnp.transpose(kernel[::-1, ::-1], (0, 1, 3, 2))


def reference(departures, error_precision, trajectory, conv_in, conv_out, hidden_bias, step_counts, obs_tiles, obs_weights, innovations, obs_precision):
    gate_factor = (1.0 - jnp.tanh(convolve(trajectory, conv_in) + hidden_bias[:, None]) ** 2).astype(jnp.bfloat16)
    gate_wide = gate_factor.astype(jnp.float32)
    back_in = flipped(conv_in)
    back_out = flipped(conv_out)

    def forward_model(current):
        for step_index in range(STEPS):
            active_mask = (step_index < step_counts)[:, None, None, None]
            hidden = (gate_wide * convolve(current.astype(jnp.bfloat16), conv_in)).astype(jnp.bfloat16)
            propagated = current + convolve(hidden, conv_out)
            current = jnp.where(active_mask, propagated, current)
        return current

    def backward_model(current):
        for step_index in range(STEPS):
            active_mask = (step_index < step_counts)[:, None, None, None]
            hidden = (gate_wide * convolve(current.astype(jnp.bfloat16), back_out)).astype(jnp.bfloat16)
            propagated = current + convolve(hidden, back_in)
            current = jnp.where(active_mask, propagated, current)
        return current

    band_base = jnp.arange(SUBWIN * N_LAT, dtype=jnp.int32).reshape(SUBWIN, N_LAT, 1) * TILES
    flat_index = (band_base + obs_tiles.reshape(SUBWIN, N_LAT, OBS_DEV).astype(jnp.int32)).reshape(-1)
    weights_flat = obs_weights.reshape(-1, TILE)

    def observe(current):
        picked = current.reshape(-1, TILE)[flat_index]
        return jnp.sum(picked * weights_flat, axis=1).reshape(SUBWIN, OBSERV)

    def observe_adjoint(scaled):
        spread_terms = weights_flat * scaled.reshape(-1)[:, None]
        tile_table = jnp.zeros((SUBWIN * N_LAT * TILES, TILE), jnp.float32).at[flat_index].add(spread_terms)
        return tile_table.reshape(SUBWIN, NROWS, C, LON)

    def shift_down(current):
        return jnp.concatenate([jnp.zeros_like(current[:1]), current[:-1]], axis=0)

    def shift_up(current):
        return jnp.concatenate([current[1:], jnp.zeros_like(current[:1])], axis=0)

    def apply_operator(direction):
        propagated = forward_model(direction)
        misfit = direction - shift_down(propagated)
        weighted = error_precision * misfit
        scaled = obs_precision * observe(propagated)
        return weighted + backward_model(observe_adjoint(scaled) - shift_up(weighted))

    first_weighted = error_precision * departures
    rhs = first_weighted + backward_model(observe_adjoint(obs_precision * innovations) - shift_up(first_weighted))
    increment = jnp.zeros_like(rhs)
    residual = rhs
    direction = rhs
    norm_now = jnp.sum(residual * residual)
    for iteration in range(ITERS):
        operator_image = apply_operator(direction)
        step_length = norm_now / jnp.sum(direction * operator_image)
        increment = increment + step_length * direction
        residual = residual - step_length * operator_image
        norm_next = jnp.sum(residual * residual)
        direction = residual + (norm_next / norm_now) * direction
        norm_now = norm_next
    return increment, residual
```

```python
import functools

import jax
import jax.numpy as jnp
from jax import lax
from jax.experimental import pallas as pl
from jax.experimental.pallas import tpu as pltpu
from jax.sharding import PartitionSpec as P

TILE = 128
STEPS = 2
ITERS = 2
F32 = jnp.float32
BF16 = jnp.bfloat16


def padded_2(cells, sides, width):
    for axis, dim in sides:
        count = lax.axis_size(axis)
        ends = count - 1
        head = lax.slice_in_dim(cells, 0, width, axis=dim)
        tail = lax.slice_in_dim(cells, cells.shape[dim] - width, cells.shape[dim], axis=dim)
        cells = jnp.concatenate(
            [
                lax.ppermute(tail, axis, [(i, (i + 1) % count) for i in range(ends)]),
                cells,
                lax.ppermute(head, axis, [((i + 1) % count, i) for i in range(ends)]),
            ],
            axis=dim,
        )
    return cells


def from_behind(value, axis, steps):
    count = lax.axis_size(axis)
    leading, last = (max(0, -steps), min(count, count - steps))
    return lax.ppermute(value, axis, [(source, source + steps) for source in range(leading, last)])


def convolve_padded(padded, kernel):
    out_rows = padded.shape[0] - 2
    lon_len = padded.shape[2]
    wrapped = jnp.concatenate([padded[:, :, -1:], padded, padded[:, :, :1]], axis=2)
    accumulated = None
    for row_off in range(3):
        for col_off in range(3):
            window = wrapped[row_off : row_off + out_rows, :, col_off : col_off + lon_len]
            term = jnp.einsum(
                "oi,ril->rol", kernel[row_off, col_off], window, preferred_element_type=F32
            )
            accumulated = term if accumulated is None else accumulated + term
    return accumulated


def flipped(kernel):
    return jnp.transpose(kernel[::-1, ::-1], (0, 1, 3, 2))


def rim_wide(source):
    return padded_2(source, (("lat", 0),), 2)


def shift_up(source):
    return from_behind(source.astype(BF16), "tm", -1).astype(source.dtype)


def global_squares(source):
    return lax.psum(jnp.sum(source * source), ("tm", "lat"))


def halo_plan(
    departures,
    error_precision,
    trajectory,
    conv_in,
    conv_out,
    hidden_bias,
    step_counts,
    obs_tiles,
    obs_weights,
    innovations,
    obs_precision,
):
    precision = error_precision[0]
    own_count = step_counts[0]
    tile_index = obs_tiles[0]
    weights = obs_weights[0]
    innovation = innovations[0]
    obs_scale = obs_precision[0]
    back_in = flipped(conv_in)
    back_out = flipped(conv_out)
    trajectory_ext = padded_2(trajectory[0], (("lat", 0),), 1)
    gate_factor = (
        1.0 - jnp.tanh(convolve_padded(trajectory_ext, conv_in) + hidden_bias[:, None]) ** 2
    ).astype(BF16)
    gate_wide = padded_2(gate_factor, (("lat", 0),), 1)

    def one_step(current, first_kernel, second_kernel):
        widened = rim_wide(current.astype(BF16))
        hidden = (gate_wide.astype(F32) * convolve_padded(widened, first_kernel)).astype(BF16)
        return current + convolve_padded(hidden, second_kernel)

    def model(current, first_kernel, second_kernel):
        for step_index in range(STEPS):
            current = jnp.where(
                step_index < own_count, one_step(current, first_kernel, second_kernel), current
            )
        return current

    def observe_adjoint(scaled, like):
        tile_table = (
            jnp.zeros((like.size // TILE, TILE), F32)
            .at[tile_index]
            .add(weights * scaled[:, None])
        )
        return tile_table.reshape(like.shape)

    first_weighted = precision * departures[0]
    rhs = first_weighted + model(
        observe_adjoint(obs_scale * innovation, first_weighted) - shift_up(first_weighted),
        back_out,
        back_in,
    )
    increment = jnp.zeros_like(rhs)
    residual = rhs
    direction = rhs
    norm_now = global_squares(residual)
    for _ in range(ITERS):
        propagated = model(direction, conv_in, conv_out)
        earlier = from_behind(propagated.astype(BF16), "tm", 1).astype(F32)
        weighted = precision * (direction - earlier)
        picked = propagated.reshape(-1, TILE)[tile_index]
        observed = jnp.sum(picked * weights, axis=1)
        operator_image = weighted + model(
            observe_adjoint(obs_scale * observed, direction) - shift_up(weighted),
            back_out,
            back_in,
        )
        curvature = lax.psum(jnp.sum(direction * operator_image), ("tm", "lat"))
        step_length = norm_now / curvature
        increment = increment + step_length * direction
        residual = residual - step_length * operator_image
        norm_next = global_squares(residual)
        direction = residual + norm_next / norm_now * direction
        norm_now = norm_next
    return (increment[None], residual[None])


BANDS = 4
CHAN = 72
CHAN_IN = 80
PAIR = 2 * CHAN
SLOTS = 4 * CHAN
EXTRA = 16


def row_of(ref, row):
    return ref[row // 2, (row % 2) * CHAN : (row % 2 + 1) * CHAN, :]


def taps_of(row):
    zeros = jnp.zeros((CHAN_IN - CHAN, row.shape[1]), F32)
    right = pltpu.roll(row, 1, axis=1)
    left = pltpu.roll(row, row.shape[1] - 1, axis=1)
    return jnp.concatenate([right, zeros, row, zeros, left, zeros], axis=0).astype(BF16)


def conv_rows(read_row, w_in, emit):
    rows = 2 * BANDS
    hid = w_in.shape[0] // 3
    sums = [None] * (rows + 1)
    for source in range(rows):
        part = jnp.dot(w_in[...], taps_of(read_row(source)), preferred_element_type=F32)
        for row_off in range(3):
            target = source + 1 - row_off
            if 0 <= target < rows:
                piece = part[row_off * hid : (row_off + 1) * hid]
                sums[target] = piece if sums[target] is None else sums[target] + piece
        if source >= 1:
            emit(source - 1, sums[source - 1])
            sums[source - 1] = None
    emit(rows - 1, sums[rows - 1])


def model_steps(field, gate, w_in, w_out, hidden, count):
    def one_step(_, carry):
        def gated(row, value):
            hidden[row] = (gate[row].astype(F32) * value).astype(BF16)

        conv_rows(lambda row: row_of(field, row), w_in, gated)
        sums = {}
        for pair in range(BANDS):
            stacked = hidden[2 * pair : 2 * pair + 2].reshape(-1, hidden.shape[2])
            part = jnp.dot(w_out[...], stacked, preferred_element_type=F32)
            for m in range(4):
                target = 2 * pair - 1 + m
                if 0 <= target < 2 * BANDS:
                    piece = part[m * 3 * CHAN : (m + 1) * 3 * CHAN]
                    sums[target] = sums[target] + piece if target in sums else piece
            done = [2 * pair - 1, 2 * pair] if pair < BANDS - 1 else [2 * pair - 1, 2 * pair, 2 * pair + 1]
            for target in done:
                if target < 0:
                    continue
                total = sums.pop(target)
                lon = total.shape[1]
                spread = (
                    pltpu.roll(total[:CHAN], 1, axis=1)
                    + total[CHAN : 2 * CHAN]
                    + pltpu.roll(total[2 * CHAN :], lon - 1, axis=1)
                )
                at = (target % 2) * CHAN
                field[target // 2, at : at + CHAN, :] = row_of(field, target) + spread
        return carry

    lax.fori_loop(0, jnp.minimum(count, STEPS), one_step, 0)


def split_16(value):
    high = value.astype(BF16)
    low = (value - high.astype(F32)).astype(BF16)
    return high, low


def extras_of(obs):
    return obs[TILE * 2 : TILE * 2 + EXTRA, :].astype(F32)


def slots_row(extra):
    halves = [2.0 * extra[h : h + 1] + extra[2 + h : 3 + h] for h in range(2)]
    return halves


def one_hot_t(halves):
    iota = lax.broadcasted_iota(jnp.int32, (SLOTS, TILE), 0).astype(F32)
    return jnp.concatenate([(iota == half).astype(F32) for half in halves], axis=1)


def one_hot(halves):
    columns = [
        jnp.transpose(jnp.broadcast_to(half, (TILE, TILE)))[:, :1] for half in halves
    ]
    column = jnp.concatenate(columns, axis=0)
    iota = lax.broadcasted_iota(jnp.int32, (2 * TILE, SLOTS), 1).astype(F32)
    return (iota == column).astype(F32)


def band_slots(band):
    return jnp.concatenate(
        [
            band[row * CHAN : (row + 1) * CHAN, half * TILE : (half + 1) * TILE]
            for row in range(2)
            for half in range(2)
        ],
        axis=0,
    )


def slots_band(slots):
    return jnp.concatenate(
        [
            jnp.concatenate(
                [slots[(2 * row + half) * CHAN : (2 * row + half + 1) * CHAN] for half in range(2)],
                axis=1,
            )
            for row in range(2)
        ],
        axis=0,
    )


def gate_kernel(t0, t1, t2, t3, w_in, bias, gate, field):
    me = lax.axis_index("lat")
    for shift, block in enumerate((t0, t1, t2, t3)):
        field[me ^ shift] = block[...].astype(F32)

    def emit(row, value):
        squashed = jnp.tanh(value + bias[...])
        gate[row] = (1.0 - squashed * squashed).astype(BF16)

    conv_rows(lambda row: row_of(field, row), w_in, emit)


def rhs_kernel(
    counts, y0, y1, y2, y3, later, o0, o1, o2, o3, gate, w_in, w_out, out, out_b, field, hidden
):
    me = lax.axis_index("lat")
    more = lax.axis_index("tm") < lax.axis_size("tm") - 1
    for shift, obs in enumerate((o0, o1, o2, o3)):
        extra = extras_of(obs)
        hot = one_hot_t(slots_row(extra))
        high = jnp.concatenate([extra[4:5], extra[5:6]], axis=1)
        low = jnp.concatenate([extra[6:7], extra[7:8]], axis=1)
        both = jnp.concatenate([hot * high, hot * low], axis=1).astype(BF16)
        weights = obs[: 2 * TILE, :]
        slots = jnp.dot(
            both, jnp.concatenate([weights, weights], axis=0), preferred_element_type=F32
        )
        next_y = jnp.where(more, later[shift].astype(F32), 0.0)
        field[me ^ shift] = slots_band(slots) - next_y
    model_steps(field, gate, w_in, w_out, hidden, counts[0])
    for shift, block in enumerate((y0, y1, y2, y3)):
        total = field[me ^ shift] + block[...].astype(F32)
        out[me ^ shift] = total
        out_b[me ^ shift] = total.astype(BF16)


def forward_kernel(counts, start, gate, w_in, w_out, out, out_b, hidden):
    out[...] = start[...]
    model_steps(out, gate, w_in, w_out, hidden, counts[0])
    out_b[...] = out[...].astype(BF16)


def observe_kernel(z, o0, o1, o2, o3, out):
    me = lax.axis_index("lat")
    for shift, obs in enumerate((o0, o1, o2, o3)):
        halves = slots_row(extras_of(obs))
        weights = obs[: 2 * TILE, :].astype(F32)
        high, low = split_16(band_slots(z[me ^ shift]))
        both = jnp.concatenate([high, low], axis=1)
        picked = jnp.dot(one_hot(halves).astype(BF16), both, preferred_element_type=F32)
        picked = picked[:, :TILE] + picked[:, TILE:]
        scaled = jnp.sum(picked * weights, axis=1, keepdims=True)
        high, low = split_16(weights * scaled)
        both = jnp.concatenate([high, low], axis=1)
        slots = jnp.dot(one_hot_t(halves).astype(BF16), both, preferred_element_type=F32)
        out[me ^ shift] = slots_band(slots[:, :TILE] + slots[:, TILE:])


def adjoint_kernel(
    counts, observed, z, later, p0, p1, p2, p3, gate, w_in, w_out, out, hidden
):
    me = lax.axis_index("lat")
    more = lax.axis_index("tm") < lax.axis_size("tm") - 1
    for shift, block in enumerate((p0, p1, p2, p3)):
        at = me ^ shift
        weight = jnp.where(more, block[...].astype(F32), 0.0)
        out[at] = observed[at] - weight * (later[at].astype(F32) - z[at])
    model_steps(out, gate, w_in, w_out, hidden, counts[0])


def image_of(at, tm_first, block, start, earlier, adjoint):
    before = jnp.where(tm_first, 0.0, earlier[at].astype(F32))
    return block[...].astype(F32) * (start[at] - before) + adjoint[at]


def image_kernel(start, earlier, adjoint, p0, p1, p2, p3, out, out_b):
    me = lax.axis_index("lat")
    tm_first = lax.axis_index("tm") == 0
    for shift, block in enumerate((p0, p1, p2, p3)):
        at = me ^ shift
        total = image_of(at, tm_first, block, start, earlier, adjoint)
        out[at] = total
        out_b[at] = total.astype(BF16)


def last_image_kernel(first, start, earlier, adjoint, p0, p1, p2, p3, own, dots):
    me = lax.axis_index("lat")
    tm_first = lax.axis_index("tm") == 0
    sums = [None] * 5
    for shift, block in enumerate((p0, p1, p2, p3)):
        at = me ^ shift
        total = image_of(at, tm_first, block, start, earlier, adjoint)
        if shift == 0:
            own[...] = total
        r0, v1 = first[at], start[at]
        for j, (a, b) in enumerate(((r0, r0), (r0, v1), (v1, v1), (r0, total), (v1, total))):
            piece = jnp.sum(a * b, axis=0, keepdims=True)
            sums[j] = piece if sums[j] is None else sums[j] + piece
    for j in range(5):
        value = jnp.sum(sums[j], axis=1, keepdims=True)
        dots[j : j + 1, :] = jnp.broadcast_to(value, (1, TILE))
    dots[5:8, :] = jnp.zeros((3, TILE), F32)


def finish_kernel(lat_at, d0, d1, d2, d3, first, second, third, inc, res):
    chan = inc.shape[1]
    lon = inc.shape[2]
    total = (d0[...] + d1[...]) + (d2[...] + d3[...])
    rr0, c0, g11, g02, g12 = [total[j : j + 1, :1] for j in range(5)]
    a0 = rr0 / c0
    rr1 = rr0 - 2.0 * a0 * c0 + a0 * a0 * g11
    beta = rr1 / rr0
    grow = 1.0 + beta
    c1 = grow * grow * c0 - grow * a0 * (g02 + g11) + a0 * a0 * g12
    a1 = rr1 / c1
    inc_r, inc_v = a0 + a1 * grow, -a1 * a0
    res_v1, res_v2 = -(a0 + a1 * grow), a1 * a0
    wide = lambda value: jnp.broadcast_to(value, (chan, lon))
    inc_r, inc_v, res_v1, res_v2 = wide(inc_r), wide(inc_v), wide(res_v1), wide(res_v2)
    for row in range(2):
        at = row * CHAN
        r0 = first[0, at : at + chan, :]
        v1 = second[0, at : at + chan, :]
        v2 = third[at : at + chan, :]
        inc[row] = inc_r * r0 + inc_v * v1
        res[row] = r0 + res_v1 * v1 + res_v2 * v2


VMEM = pl.BlockSpec(memory_space=pltpu.VMEM)
SMEM = pl.BlockSpec(memory_space=pltpu.SMEM)


def call(kernel, name, ins, outs, scratch=(), scalars=0):
    specs = [SMEM] * scalars + [VMEM] * (len(ins) - scalars)
    return pl.pallas_call(
        kernel,
        name=name,
        out_shape=outs,
        in_specs=specs,
        out_specs=[VMEM] * len(outs),
        scratch_shapes=list(scratch),
        compiler_params=pltpu.CompilerParams(vmem_limit_bytes=48 << 20),
    )(*ins)


def stack_in(kernel):
    rows, cols, out_c, in_c = kernel.shape
    padded = jnp.pad(kernel, ((0, 0), (0, 0), (0, 0), (0, CHAN_IN - in_c)))
    return jnp.transpose(padded, (0, 2, 1, 3)).reshape(rows * out_c, cols * CHAN_IN)


def stack_out(kernel):
    rows, cols, out_c, in_c = kernel.shape
    padded = jnp.pad(kernel, ((0, 0), (0, 0), (0, CHAN - out_c), (0, 0)))
    none = jnp.zeros_like(padded[0])
    tap = lambda row_off: padded[row_off] if 0 <= row_off < rows else none
    blocks = [jnp.concatenate([tap(2 - m), tap(3 - m)], axis=-1) for m in range(4)]
    return jnp.concatenate(blocks, axis=0).reshape(4 * cols * CHAN, 2 * in_c)


def as_band(cells):
    rows, chan, lon = cells.shape
    return jnp.pad(cells.astype(BF16), ((0, 0), (0, CHAN - chan), (0, 0))).reshape(PAIR, lon)


def by_partner(value):
    count = lax.axis_size("lat")
    blocks = [value]
    for shift in range(1, count):
        blocks.append(lax.ppermute(value, "lat", [(i, i ^ shift) for i in range(count)]))
    return blocks


def along_tm(value, step):
    count = lax.axis_size("tm")
    return lax.ppermute(value, "tm", [(i, (i + step) % count) for i in range(count)])


def row_plan(
    departures,
    error_precision,
    trajectory,
    conv_in,
    conv_out,
    hidden_bias,
    step_counts,
    obs_tiles,
    obs_weights,
    innovations,
    obs_precision,
):
    _, rows, chan, lon = departures.shape
    hid = conv_in.shape[2]
    shape = lambda *dims: jax.ShapeDtypeStruct(dims, F32)
    shape_b = lambda *dims: jax.ShapeDtypeStruct(dims, BF16)
    whole, whole_b = shape(BANDS, PAIR, lon), shape_b(BANDS, PAIR, lon)

    y_own = as_band(error_precision[0] * departures[0])
    y_all = by_partner(y_own)
    t_all = by_partner(as_band(trajectory[0]))

    root = jnp.sqrt(obs_precision[0])
    tiles = obs_tiles[0]
    per_row = 2 * chan
    slot = (2 * (tiles // per_row) + tiles % 2) * CHAN + (tiles // 2) % chan
    innov_high, innov_low = split_16(root * innovations[0])
    table = lambda value: value.astype(BF16).reshape(-1, TILE)
    obs_own = jnp.concatenate(
        [
            (obs_weights[0] * root[:, None]).astype(BF16),
            table(slot // 2),
            table(slot % 2),
            table(innov_high),
            table(innov_low),
            jnp.zeros((EXTRA - 8, TILE), BF16),
        ],
        axis=0,
    )
    o_all = by_partner(obs_own)
    p_all = by_partner(as_band(error_precision[0]))
    y_later = along_tm(jnp.stack(y_all), -1)
    p_later = [along_tm(block, -1) for block in p_all]

    fore_in, fore_out = stack_in(conv_in), stack_out(conv_out)
    back_in, back_out = stack_in(flipped(conv_out)), stack_out(flipped(conv_in))
    hidden = pltpu.VMEM((rows * BANDS, hid, lon), BF16)
    field = pltpu.VMEM((BANDS, PAIR, lon), F32)

    (gate,) = call(
        gate_kernel,
        "gate",
        (*t_all, fore_in, hidden_bias[:, None]),
        [shape_b(rows * BANDS, hid, lon)],
        [field],
    )
    r0, r0_b = call(
        rhs_kernel,
        "rhs",
        (step_counts, *y_all, y_later, *o_all, gate, back_in, back_out),
        [whole, whole_b],
        [field, hidden],
        1,
    )

    def half(start, start_b):
        later = along_tm(start_b, -1)
        z, z_b = call(
            forward_kernel,
            "forward",
            (step_counts, start, gate, fore_in, fore_out),
            [whole, whole_b],
            [hidden],
            1,
        )
        earlier = along_tm(z_b, 1)
        (observed,) = call(observe_kernel, "observe", (z, *o_all), [whole])
        (adjoint,) = call(
            adjoint_kernel,
            "adjoint",
            (step_counts, observed, z, later, *p_later, gate, back_in, back_out),
            [whole],
            [hidden],
            1,
        )
        return earlier, adjoint

    earlier, adjoint = half(r0, r0_b)
    v1, v1_b = call(image_kernel, "image", (r0, earlier, adjoint, *p_all), [whole, whole_b])
    earlier, adjoint = half(v1, v1_b)
    own, dots = call(
        last_image_kernel,
        "last_image",
        (r0, v1, earlier, adjoint, *p_all),
        [shape(PAIR, lon), shape(8, TILE)],
    )
    count = lax.axis_size("tm")
    parts = [dots] + [
        lax.ppermute(dots, "tm", [(i, i ^ step) for i in range(count)]) for step in range(1, count)
    ]
    at = lax.axis_index("lat").astype(jnp.int32).reshape(1)
    small = pl.BlockSpec((8, TILE), lambda g, lat_at: (0, 0))
    band = pl.BlockSpec((1, PAIR, lon), lambda g, lat_at: (lat_at[0], 0, 0))
    out_block = pl.BlockSpec((rows, chan, lon), lambda g, lat_at: (0, 0, 0))
    inc, res = pl.pallas_call(
        finish_kernel,
        name="finish",
        grid_spec=pltpu.PrefetchScalarGridSpec(
            num_scalar_prefetch=1,
            grid=(1,),
            in_specs=[small] * 4 + [band, band, pl.BlockSpec((PAIR, lon), lambda g, lat_at: (0, 0))],
            out_specs=[out_block, out_block],
        ),
        out_shape=[shape(rows, chan, lon)] * 2,
    )(at, *parts, r0, v1, own)
    return (inc[None], res[None])


def solution(mesh):
    in_specs = (
        P(("ens", "tm"), "lat", None, None),
        P(("ens", "tm"), "lat", None, None),
        P(("ens", "tm"), "lat", None, None),
        P(),
        P(),
        P(),
        P(("ens", "tm")),
        P(("ens", "tm"), "lat"),
        P(("ens", "tm"), "lat", None),
        P(("ens", "tm"), "lat"),
        P(("ens", "tm"), "lat"),
    )
    out_specs = (P(("ens", "tm"), "lat", None, None), P(("ens", "tm"), "lat", None, None))
    plan = row_plan if mesh.shape["lat"] == BANDS and mesh.shape["tm"] == 4 else halo_plan
    return jax.shard_map(plan, mesh=mesh, in_specs=in_specs, out_specs=out_specs, check_vma=False)
```

```python
import functools

import jax
import jax.numpy as jnp
from jax import lax
from jax.experimental import pallas as pl
from jax.experimental.pallas import tpu as pltpu
from jax.sharding import PartitionSpec as P

TILE = 128
STEPS = 2
ITERS = 2
F32 = jnp.float32
BF16 = jnp.bfloat16


def padded_2(cells, sides, width):
    for axis, dim in sides:
        count = lax.axis_size(axis)
        ends = count - 1
        head = lax.slice_in_dim(cells, 0, width, axis=dim)
        tail = lax.slice_in_dim(cells, cells.shape[dim] - width, cells.shape[dim], axis=dim)
        cells = jnp.concatenate(
            [
                lax.ppermute(tail, axis, [(i, (i + 1) % count) for i in range(ends)]),
                cells,
                lax.ppermute(head, axis, [((i + 1) % count, i) for i in range(ends)]),
            ],
            axis=dim,
        )
    return cells


def from_behind(value, axis, steps):
    count = lax.axis_size(axis)
    leading, last = (max(0, -steps), min(count, count - steps))
    return lax.ppermute(value, axis, [(source, source + steps) for source in range(leading, last)])


def convolve_padded(padded, kernel):
    out_rows = padded.shape[0] - 2
    lon_len = padded.shape[2]
    wrapped = jnp.concatenate([padded[:, :, -1:], padded, padded[:, :, :1]], axis=2)
    accumulated = None
    for row_off in range(3):
        for col_off in range(3):
            window = wrapped[row_off : row_off + out_rows, :, col_off : col_off + lon_len]
            term = jnp.einsum(
                "oi,ril->rol", kernel[row_off, col_off], window, preferred_element_type=F32
            )
            accumulated = term if accumulated is None else accumulated + term
    return accumulated


def flipped(kernel):
    return jnp.transpose(kernel[::-1, ::-1], (0, 1, 3, 2))


def rim_wide(source):
    return padded_2(source, (("lat", 0),), 2)


def shift_up(source):
    return from_behind(source.astype(BF16), "tm", -1).astype(source.dtype)


def global_squares(source):
    return lax.psum(jnp.sum(source * source), ("tm", "lat"))


def halo_plan(
    departures,
    error_precision,
    trajectory,
    conv_in,
    conv_out,
    hidden_bias,
    step_counts,
    obs_tiles,
    obs_weights,
    innovations,
    obs_precision,
):
    precision = error_precision[0]
    own_count = step_counts[0]
    tile_index = obs_tiles[0]
    weights = obs_weights[0]
    innovation = innovations[0]
    obs_scale = obs_precision[0]
    back_in = flipped(conv_in)
    back_out = flipped(conv_out)
    trajectory_ext = padded_2(trajectory[0], (("lat", 0),), 1)
    gate_factor = (
        1.0 - jnp.tanh(convolve_padded(trajectory_ext, conv_in) + hidden_bias[:, None]) ** 2
    ).astype(BF16)
    gate_wide = padded_2(gate_factor, (("lat", 0),), 1)

    def one_step(current, first_kernel, second_kernel):
        widened = rim_wide(current.astype(BF16))
        hidden = (gate_wide.astype(F32) * convolve_padded(widened, first_kernel)).astype(BF16)
        return current + convolve_padded(hidden, second_kernel)

    def model(current, first_kernel, second_kernel):
        for step_index in range(STEPS):
            current = jnp.where(
                step_index < own_count, one_step(current, first_kernel, second_kernel), current
            )
        return current

    def observe_adjoint(scaled, like):
        tile_table = (
            jnp.zeros((like.size // TILE, TILE), F32)
            .at[tile_index]
            .add(weights * scaled[:, None])
        )
        return tile_table.reshape(like.shape)

    first_weighted = precision * departures[0]
    rhs = first_weighted + model(
        observe_adjoint(obs_scale * innovation, first_weighted) - shift_up(first_weighted),
        back_out,
        back_in,
    )
    increment = jnp.zeros_like(rhs)
    residual = rhs
    direction = rhs
    norm_now = global_squares(residual)
    for _ in range(ITERS):
        propagated = model(direction, conv_in, conv_out)
        earlier = from_behind(propagated.astype(BF16), "tm", 1).astype(F32)
        weighted = precision * (direction - earlier)
        picked = propagated.reshape(-1, TILE)[tile_index]
        observed = jnp.sum(picked * weights, axis=1)
        operator_image = weighted + model(
            observe_adjoint(obs_scale * observed, direction) - shift_up(weighted),
            back_out,
            back_in,
        )
        curvature = lax.psum(jnp.sum(direction * operator_image), ("tm", "lat"))
        step_length = norm_now / curvature
        increment = increment + step_length * direction
        residual = residual - step_length * operator_image
        norm_next = global_squares(residual)
        direction = residual + norm_next / norm_now * direction
        norm_now = norm_next
    return (increment[None], residual[None])


BANDS = 4
ROWS = 2 * BANDS
CHAN = 72
CHAN_IN = 80
TAPS = 256
PAIR = 2 * CHAN
SLOTS = 4 * CHAN
OBS_ROWS = 144


def row_of(ref, row):
    return ref[row // 2, (row % 2) * CHAN : (row % 2 + 1) * CHAN, :]


def taps_of(row):
    zeros = jnp.zeros((CHAN_IN - CHAN, row.shape[1]), F32)
    right = pltpu.roll(row, 1, axis=1)
    left = pltpu.roll(row, row.shape[1] - 1, axis=1)
    return jnp.concatenate([right, zeros, row, zeros, left, zeros], axis=0).astype(BF16)


def clear_taps(taps):
    used = 3 * CHAN_IN
    taps[:, used:, :] = jnp.zeros((ROWS, TAPS - used, taps.shape[2]), BF16)


def conv_rows(field, w_in, taps, emit):
    for row in range(ROWS):
        taps[row, : 3 * CHAN_IN] = taps_of(row_of(field, row))
    for row in range(ROWS):
        low, high = max(row - 1, 0), min(row + 2, ROWS)
        stacked = taps[low:high].reshape((high - low) * TAPS, taps.shape[2])
        skip = (low - (row - 1)) * TAPS
        weights = w_in[:, skip : skip + (high - low) * TAPS]
        emit(row, jnp.dot(weights, stacked, preferred_element_type=F32))


def model_steps(field, gate, w_in, w_out, taps, hidden, count):
    clear_taps(taps)
    hidden[0] = jnp.zeros(hidden.shape[1:], BF16)
    hidden[ROWS + 1] = jnp.zeros(hidden.shape[1:], BF16)

    def gated(row, value):
        hidden[row + 1] = (gate[row].astype(F32) * value).astype(BF16)

    def one_step(_, carry):
        conv_rows(field, w_in, taps, gated)
        for pair in range(BANDS):
            stacked = hidden[2 * pair : 2 * pair + 4].reshape(-1, hidden.shape[2])
            part = jnp.dot(w_out[...], stacked, preferred_element_type=F32)
            lon = part.shape[1]
            for row in range(2):
                tap = [part[(3 * row + b) * CHAN : (3 * row + b + 1) * CHAN] for b in range(3)]
                spread = pltpu.roll(tap[0], 1, axis=1) + tap[1] + pltpu.roll(tap[2], lon - 1, axis=1)
                at = row * CHAN
                field[pair, at : at + CHAN, :] = field[pair, at : at + CHAN, :] + spread
        return carry

    lax.fori_loop(0, jnp.minimum(count, STEPS), one_step, 0)


def split_16(value):
    high = value.astype(BF16)
    low = (value - high.astype(F32)).astype(BF16)
    return high, low


def obs_of(obs):
    weights = jnp.concatenate([obs[:TILE, :TILE], obs[:TILE, TILE:]], axis=0)
    extra = obs[TILE:, :].astype(F32)
    return weights, 2.0 * extra[0:1] + extra[1:2], extra[2:3], extra[3:4]


def one_hot_t(slot):
    iota = lax.broadcasted_iota(jnp.int32, (SLOTS, 2 * TILE), 0).astype(F32)
    return (iota == slot).astype(F32)


def one_hot(slot):
    columns = [
        jnp.transpose(jnp.broadcast_to(slot[:, half * TILE : (half + 1) * TILE], (TILE, TILE)))[:, :1]
        for half in range(2)
    ]
    column = jnp.concatenate(columns, axis=0)
    iota = lax.broadcasted_iota(jnp.int32, (2 * TILE, SLOTS), 1).astype(F32)
    return (iota == column).astype(F32)


def band_slots(band):
    return jnp.concatenate(
        [
            band[row * CHAN : (row + 1) * CHAN, half * TILE : (half + 1) * TILE]
            for row in range(2)
            for half in range(2)
        ],
        axis=0,
    )


def slots_band(slots):
    return jnp.concatenate(
        [
            jnp.concatenate(
                [slots[(2 * row + half) * CHAN : (2 * row + half + 1) * CHAN] for half in range(2)],
                axis=1,
            )
            for row in range(2)
        ],
        axis=0,
    )


def gate_kernel(b0, b1, b2, b3, w_in, bias, gate, field, taps):
    me = lax.axis_index("lat")
    for shift, block in enumerate((b0, b1, b2, b3)):
        field[me ^ shift] = block[0].astype(F32)
    clear_taps(taps)

    def emit(row, value):
        squashed = jnp.tanh(value + bias[...])
        gate[row] = (1.0 - squashed * squashed).astype(BF16)

    conv_rows(field, w_in, taps, emit)


def rhs_kernel(
    counts, y0, y1, y2, y3, later, b0, b1, b2, b3, gate, w_in, w_out, out, out_b, field, taps, hidden
):
    me = lax.axis_index("lat")
    more = lax.axis_index("tm") < lax.axis_size("tm") - 1
    for shift, block in enumerate((b0, b1, b2, b3)):
        weights, slot, high, low = obs_of(block[1])
        hot = one_hot_t(slot)
        both = jnp.concatenate([hot * high, hot * low], axis=1).astype(BF16)
        slots = jnp.dot(
            both, jnp.concatenate([weights, weights], axis=0), preferred_element_type=F32
        )
        next_y = jnp.where(more, later[shift].astype(F32), 0.0)
        field[me ^ shift] = slots_band(slots) - next_y
    model_steps(field, gate, w_in, w_out, taps, hidden, counts[0])
    for shift, block in enumerate((y0, y1, y2, y3)):
        total = field[me ^ shift] + block[...].astype(F32)
        out[me ^ shift] = total
        out_b[me ^ shift] = total.astype(BF16)


def forward_kernel(counts, start, gate, w_in, w_out, out, out_b, taps, hidden):
    out[...] = start[...]
    model_steps(out, gate, w_in, w_out, taps, hidden, counts[0])
    out_b[...] = out[...].astype(BF16)


def observe_kernel(z, b0, b1, b2, b3, out):
    me = lax.axis_index("lat")
    for shift, block in enumerate((b0, b1, b2, b3)):
        weights, slot, _, _ = obs_of(block[1])
        weights = weights.astype(F32)
        high, low = split_16(band_slots(z[me ^ shift]))
        both = jnp.concatenate([high, low], axis=1)
        picked = jnp.dot(one_hot(slot).astype(BF16), both, preferred_element_type=F32)
        picked = picked[:, :TILE] + picked[:, TILE:]
        scaled = jnp.sum(picked * weights, axis=1, keepdims=True)
        high, low = split_16(weights * scaled)
        both = jnp.concatenate([high, low], axis=1)
        slots = jnp.dot(one_hot_t(slot).astype(BF16), both, preferred_element_type=F32)
        out[me ^ shift] = slots_band(slots[:, :TILE] + slots[:, TILE:])


def adjoint_kernel(
    counts, observed, z, later, precision, gate, w_in, w_out, out, taps, hidden
):
    me = lax.axis_index("lat")
    more = lax.axis_index("tm") < lax.axis_size("tm") - 1
    for shift in range(BANDS):
        at = me ^ shift
        weight = jnp.where(more, precision[shift].astype(F32), 0.0)
        out[at] = observed[at] - weight * (later[at].astype(F32) - z[at])
    model_steps(out, gate, w_in, w_out, taps, hidden, counts[0])


def image_of(at, tm_first, block, start, earlier, adjoint):
    before = jnp.where(tm_first, 0.0, earlier[at].astype(F32))
    return block[...].astype(F32) * (start[at] - before) + adjoint[at]


def image_kernel(start, earlier, adjoint, p0, p1, p2, p3, out, out_b):
    me = lax.axis_index("lat")
    tm_first = lax.axis_index("tm") == 0
    for shift, block in enumerate((p0, p1, p2, p3)):
        at = me ^ shift
        total = image_of(at, tm_first, block, start, earlier, adjoint)
        out[at] = total
        out_b[at] = total.astype(BF16)


def last_image_kernel(first, start, earlier, adjoint, p0, p1, p2, p3, own, dots):
    me = lax.axis_index("lat")
    tm_first = lax.axis_index("tm") == 0
    sums = [None] * 5
    for shift, block in enumerate((p0, p1, p2, p3)):
        at = me ^ shift
        total = image_of(at, tm_first, block, start, earlier, adjoint)
        if shift == 0:
            own[...] = total
        r0, v1 = first[at], start[at]
        for j, (a, b) in enumerate(((r0, r0), (r0, v1), (v1, v1), (r0, total), (v1, total))):
            piece = jnp.sum(a * b, axis=0, keepdims=True)
            sums[j] = piece if sums[j] is None else sums[j] + piece
    for j in range(5):
        value = jnp.sum(sums[j], axis=1, keepdims=True)
        dots[j : j + 1, :] = jnp.broadcast_to(value, (1, TILE))
    dots[5:8, :] = jnp.zeros((3, TILE), F32)


def finish_kernel(d0, d1, d2, d3, first, second, third, inc, res):
    me = lax.axis_index("lat")
    chan, _, lon = inc.shape
    total = (d0[...] + d1[...]) + (d2[...] + d3[...])
    rr0, c0, g11, g02, g12 = [total[j : j + 1, :1] for j in range(5)]
    a0 = rr0 / c0
    rr1 = rr0 - 2.0 * a0 * c0 + a0 * a0 * g11
    beta = rr1 / rr0
    grow = 1.0 + beta
    c1 = grow * grow * c0 - grow * a0 * (g02 + g11) + a0 * a0 * g12
    a1 = rr1 / c1
    wide = lambda value: jnp.broadcast_to(value, (chan, lon))
    inc_r, cross, twice = wide(a0 + a1 * grow), wide(a1 * a0), wide(a0 + a1 * grow)
    for row in range(2):
        at = row * CHAN
        r0 = first[me, at : at + chan, :]
        v1 = second[me, at : at + chan, :]
        v2 = third[at : at + chan, :]
        inc[:, row, :] = inc_r * r0 - cross * v1
        res[:, row, :] = r0 - twice * v1 + cross * v2


VMEM = pl.BlockSpec(memory_space=pltpu.VMEM)
SMEM = pl.BlockSpec(memory_space=pltpu.SMEM)


def call(kernel, name, ins, outs, scratch=(), scalars=0):
    specs = [SMEM] * scalars + [VMEM] * (len(ins) - scalars)
    return pl.pallas_call(
        kernel,
        name=name,
        out_shape=outs,
        in_specs=specs,
        out_specs=[VMEM] * len(outs),
        scratch_shapes=list(scratch),
        compiler_params=pltpu.CompilerParams(vmem_limit_bytes=48 << 20),
        cost_estimate=pl.CostEstimate(flops=1, bytes_accessed=1, transcendentals=0),
    )(*ins)


def stack_in(kernel):
    rows, cols, out_c, in_c = kernel.shape
    padded = jnp.pad(kernel, ((0, 0), (0, 0), (0, 0), (0, CHAN_IN - in_c)))
    block = jnp.transpose(padded, (2, 0, 1, 3)).reshape(out_c, rows, cols * CHAN_IN)
    block = jnp.pad(block, ((0, 0), (0, 0), (0, TAPS - cols * CHAN_IN)))
    return block.reshape(out_c, rows * TAPS)


def stack_out(kernel):
    rows, cols, out_c, in_c = kernel.shape
    padded = jnp.pad(kernel, ((0, 0), (0, 0), (0, CHAN - out_c), (0, 0)))
    none = jnp.zeros_like(padded[0])
    tap = lambda row_off: padded[row_off] if 0 <= row_off < rows else none
    blocks = [jnp.concatenate([tap(t - m) for t in range(4)], axis=-1) for m in range(2)]
    return jnp.concatenate(blocks, axis=0).reshape(2 * cols * CHAN, 4 * in_c)


def as_band(cells):
    rows, chan, lon = cells.shape
    return jnp.pad(cells.astype(BF16), ((0, 0), (0, CHAN - chan), (0, 0))).reshape(PAIR, lon)


def by_partner(value):
    swap = lambda block, shift: lax.ppermute(
        block, "lat", [(i, i ^ shift) for i in range(lax.axis_size("lat"))]
    )
    far = swap(value, 2)
    return [value, swap(value, 1), far, swap(far, 1)]


def along_tm(value, step):
    count = lax.axis_size("tm")
    return lax.ppermute(value, "tm", [(i, (i + step) % count) for i in range(count)])


def row_plan(
    departures,
    error_precision,
    trajectory,
    conv_in,
    conv_out,
    hidden_bias,
    step_counts,
    obs_tiles,
    obs_weights,
    innovations,
    obs_precision,
):
    _, rows, chan, lon = departures.shape
    hid = conv_in.shape[2]
    shape = lambda *dims: jax.ShapeDtypeStruct(dims, F32)
    shape_b = lambda *dims: jax.ShapeDtypeStruct(dims, BF16)
    whole, whole_b = shape(BANDS, PAIR, lon), shape_b(BANDS, PAIR, lon)

    root = jnp.sqrt(obs_precision[0])
    tiles = obs_tiles[0]
    per_row = 2 * chan
    slot = (2 * (tiles // per_row) + tiles % 2) * CHAN + (tiles // 2) % chan
    innov_high, innov_low = split_16(root * innovations[0])
    table = lambda value: value.astype(BF16).reshape(1, 2 * TILE)
    weights = (obs_weights[0] * root[:, None]).astype(BF16)
    obs_own = jnp.concatenate(
        [
            jnp.concatenate([weights[:TILE], weights[TILE:]], axis=1),
            table(slot // 2),
            table(slot % 2),
            table(innov_high),
            table(innov_low),
            jnp.zeros((OBS_ROWS - TILE - 4, 2 * TILE), BF16),
        ],
        axis=0,
    )
    both_own = jnp.stack([as_band(trajectory[0]), obs_own])
    prec_own = as_band(error_precision[0])

    y_all = by_partner(as_band(error_precision[0] * departures[0]))
    both_own, _ = lax.optimization_barrier((both_own, y_all[2]))
    b_all = by_partner(both_own)
    prec_own, _ = lax.optimization_barrier((prec_own, b_all[2]))
    p_all = by_partner(prec_own)
    y_later = along_tm(jnp.stack(y_all), -1)
    p_later = along_tm(jnp.stack(p_all), -1)

    fore_in, fore_out = stack_in(conv_in), stack_out(conv_out)
    back_in, back_out = stack_in(flipped(conv_out)), stack_out(flipped(conv_in))
    taps = pltpu.VMEM((ROWS, TAPS, lon), BF16)
    hidden = pltpu.VMEM((ROWS + 2, hid, lon), BF16)
    field = pltpu.VMEM((BANDS, PAIR, lon), F32)

    (gate,) = call(
        gate_kernel,
        "gate",
        (*b_all, fore_in, hidden_bias[:, None]),
        [shape_b(ROWS, hid, lon)],
        [field, taps],
    )
    r0, r0_b = call(
        rhs_kernel,
        "rhs",
        (step_counts, *y_all, y_later, *b_all, gate, back_in, back_out),
        [whole, whole_b],
        [field, taps, hidden],
        1,
    )

    def half(start, start_b):
        later = along_tm(start_b, -1)
        z, z_b = call(
            forward_kernel,
            "forward",
            (step_counts, start, gate, fore_in, fore_out),
            [whole, whole_b],
            [taps, hidden],
            1,
        )
        earlier = along_tm(z_b, 1)
        (observed,) = call(observe_kernel, "observe", (z, *b_all), [whole])
        (adjoint,) = call(
            adjoint_kernel,
            "adjoint",
            (step_counts, observed, z, later, p_later, gate, back_in, back_out),
            [whole],
            [taps, hidden],
            1,
        )
        return earlier, adjoint

    earlier, adjoint = half(r0, r0_b)
    v1, v1_b = call(image_kernel, "image", (r0, earlier, adjoint, *p_all), [whole, whole_b])
    earlier, adjoint = half(v1, v1_b)
    own, dots = call(
        last_image_kernel,
        "last_image",
        (r0, v1, earlier, adjoint, *p_all),
        [shape(PAIR, lon), shape(8, TILE)],
    )
    count = lax.axis_size("tm")
    parts = [dots] + [
        lax.ppermute(dots, "tm", [(i, i ^ step) for i in range(count)]) for step in range(1, count)
    ]
    inc, res = call(
        finish_kernel, "finish", (*parts, r0, v1, own), [shape(chan, rows, lon)] * 2
    )
    return (jnp.transpose(inc, (1, 0, 2))[None], jnp.transpose(res, (1, 0, 2))[None])


def solution(mesh):
    in_specs = (
        P(("ens", "tm"), "lat", None, None),
        P(("ens", "tm"), "lat", None, None),
        P(("ens", "tm"), "lat", None, None),
        P(),
        P(),
        P(),
        P(("ens", "tm")),
        P(("ens", "tm"), "lat"),
        P(("ens", "tm"), "lat", None),
        P(("ens", "tm"), "lat"),
        P(("ens", "tm"), "lat"),
    )
    out_specs = (P(("ens", "tm"), "lat", None, None), P(("ens", "tm"), "lat", None, None))
    plan = row_plan if mesh.shape["lat"] == BANDS and mesh.shape["tm"] == 4 else halo_plan
    return jax.shard_map(plan, mesh=mesh, in_specs=in_specs, out_specs=out_specs, check_vma=False)
```

```python
import functools

import jax
import jax.numpy as jnp
from jax import lax
from jax.experimental import pallas as pl
from jax.experimental.pallas import tpu as pltpu
from jax.sharding import PartitionSpec as P

TILE = 128
STEPS = 2
ITERS = 2
F32 = jnp.float32
BF16 = jnp.bfloat16


def padded_2(cells, sides, width):
    for axis, dim in sides:
        count = lax.axis_size(axis)
        ends = count - 1
        head = lax.slice_in_dim(cells, 0, width, axis=dim)
        tail = lax.slice_in_dim(cells, cells.shape[dim] - width, cells.shape[dim], axis=dim)
        cells = jnp.concatenate(
            [
                lax.ppermute(tail, axis, [(i, (i + 1) % count) for i in range(ends)]),
                cells,
                lax.ppermute(head, axis, [((i + 1) % count, i) for i in range(ends)]),
            ],
            axis=dim,
        )
    return cells


def from_behind(value, axis, steps):
    count = lax.axis_size(axis)
    leading, last = (max(0, -steps), min(count, count - steps))
    return lax.ppermute(value, axis, [(source, source + steps) for source in range(leading, last)])


def convolve_padded(padded, kernel):
    out_rows = padded.shape[0] - 2
    lon_len = padded.shape[2]
    wrapped = jnp.concatenate([padded[:, :, -1:], padded, padded[:, :, :1]], axis=2)
    accumulated = None
    for row_off in range(3):
        for col_off in range(3):
            window = wrapped[row_off : row_off + out_rows, :, col_off : col_off + lon_len]
            term = jnp.einsum(
                "oi,ril->rol", kernel[row_off, col_off], window, preferred_element_type=F32
            )
            accumulated = term if accumulated is None else accumulated + term
    return accumulated


def flipped(kernel):
    return jnp.transpose(kernel[::-1, ::-1], (0, 1, 3, 2))


def rim_wide(source):
    return padded_2(source, (("lat", 0),), 2)


def shift_up(source):
    return from_behind(source.astype(BF16), "tm", -1).astype(source.dtype)


def global_squares(source):
    return lax.psum(jnp.sum(source * source), ("tm", "lat"))


def halo_plan(
    departures,
    error_precision,
    trajectory,
    conv_in,
    conv_out,
    hidden_bias,
    step_counts,
    obs_tiles,
    obs_weights,
    innovations,
    obs_precision,
):
    precision = error_precision[0]
    own_count = step_counts[0]
    tile_index = obs_tiles[0]
    weights = obs_weights[0]
    innovation = innovations[0]
    obs_scale = obs_precision[0]
    back_in = flipped(conv_in)
    back_out = flipped(conv_out)
    trajectory_ext = padded_2(trajectory[0], (("lat", 0),), 1)
    gate_factor = (
        1.0 - jnp.tanh(convolve_padded(trajectory_ext, conv_in) + hidden_bias[:, None]) ** 2
    ).astype(BF16)
    gate_wide = padded_2(gate_factor, (("lat", 0),), 1)

    def one_step(current, first_kernel, second_kernel):
        widened = rim_wide(current.astype(BF16))
        hidden = (gate_wide.astype(F32) * convolve_padded(widened, first_kernel)).astype(BF16)
        return current + convolve_padded(hidden, second_kernel)

    def model(current, first_kernel, second_kernel):
        for step_index in range(STEPS):
            current = jnp.where(
                step_index < own_count, one_step(current, first_kernel, second_kernel), current
            )
        return current

    def observe_adjoint(scaled, like):
        tile_table = (
            jnp.zeros((like.size // TILE, TILE), F32)
            .at[tile_index]
            .add(weights * scaled[:, None])
        )
        return tile_table.reshape(like.shape)

    first_weighted = precision * departures[0]
    rhs = first_weighted + model(
        observe_adjoint(obs_scale * innovation, first_weighted) - shift_up(first_weighted),
        back_out,
        back_in,
    )
    increment = jnp.zeros_like(rhs)
    residual = rhs
    direction = rhs
    norm_now = global_squares(residual)
    for _ in range(ITERS):
        propagated = model(direction, conv_in, conv_out)
        earlier = from_behind(propagated.astype(BF16), "tm", 1).astype(F32)
        weighted = precision * (direction - earlier)
        picked = propagated.reshape(-1, TILE)[tile_index]
        observed = jnp.sum(picked * weights, axis=1)
        operator_image = weighted + model(
            observe_adjoint(obs_scale * observed, direction) - shift_up(weighted),
            back_out,
            back_in,
        )
        curvature = lax.psum(jnp.sum(direction * operator_image), ("tm", "lat"))
        step_length = norm_now / curvature
        increment = increment + step_length * direction
        residual = residual - step_length * operator_image
        norm_next = global_squares(residual)
        direction = residual + norm_next / norm_now * direction
        norm_now = norm_next
    return (increment[None], residual[None])


BANDS = 4
ROWS = 2 * BANDS
CHAN = 72
CHAN_IN = 80
TAPS = 256
PAIR = 2 * CHAN
SLOTS = 4 * CHAN
OBS_ROWS = 144


def row_of(ref, row):
    return ref[row // 2, (row % 2) * CHAN : (row % 2 + 1) * CHAN, :]


def taps_of(row):
    zeros = jnp.zeros((CHAN_IN - CHAN, row.shape[1]), F32)
    right = pltpu.roll(row, 1, axis=1)
    left = pltpu.roll(row, row.shape[1] - 1, axis=1)
    return jnp.concatenate([right, zeros, row, zeros, left, zeros], axis=0).astype(BF16)


def clear_taps(taps):
    used = 3 * CHAN_IN
    taps[:, used:, :] = jnp.zeros((ROWS, TAPS - used, taps.shape[2]), BF16)


def conv_rows(field, w_in, taps, emit):
    for row in range(ROWS):
        taps[row, : 3 * CHAN_IN] = taps_of(row_of(field, row))
    for row in range(ROWS):
        low, high = max(row - 1, 0), min(row + 2, ROWS)
        stacked = taps[low:high].reshape((high - low) * TAPS, taps.shape[2])
        skip = (low - (row - 1)) * TAPS
        weights = w_in[:, skip : skip + (high - low) * TAPS]
        emit(row, jnp.dot(weights, stacked, preferred_element_type=F32))


def model_steps(field, gate, w_in, w_out, taps, hidden, count):
    clear_taps(taps)
    hidden[0] = jnp.zeros(hidden.shape[1:], BF16)
    hidden[ROWS + 1] = jnp.zeros(hidden.shape[1:], BF16)

    def gated(row, value):
        hidden[row + 1] = (gate[row].astype(F32) * value).astype(BF16)

    def one_step(_, carry):
        conv_rows(field, w_in, taps, gated)
        for pair in range(BANDS):
            stacked = hidden[2 * pair : 2 * pair + 4].reshape(-1, hidden.shape[2])
            part = jnp.dot(w_out[...], stacked, preferred_element_type=F32)
            lon = part.shape[1]
            for row in range(2):
                tap = [part[(3 * row + b) * CHAN : (3 * row + b + 1) * CHAN] for b in range(3)]
                spread = pltpu.roll(tap[0], 1, axis=1) + tap[1] + pltpu.roll(tap[2], lon - 1, axis=1)
                at = row * CHAN
                field[pair, at : at + CHAN, :] = field[pair, at : at + CHAN, :] + spread
        return carry

    lax.fori_loop(0, jnp.minimum(count, STEPS), one_step, 0)


def split_16(value):
    high = value.astype(BF16)
    low = (value - high.astype(F32)).astype(BF16)
    return high, low


def obs_of(obs):
    weights = jnp.concatenate([obs[:TILE, :TILE], obs[:TILE, TILE:]], axis=0)
    extra = obs[TILE:, :].astype(F32)
    return weights, 2.0 * extra[0:1] + extra[1:2], extra[2:3], extra[3:4]


def one_hot_t(slot):
    iota = lax.broadcasted_iota(jnp.int32, (SLOTS, 2 * TILE), 0).astype(F32)
    return (iota == slot).astype(F32)


def one_hot(slot):
    columns = [
        jnp.transpose(jnp.broadcast_to(slot[:, half * TILE : (half + 1) * TILE], (TILE, TILE)))[:, :1]
        for half in range(2)
    ]
    column = jnp.concatenate(columns, axis=0)
    iota = lax.broadcasted_iota(jnp.int32, (2 * TILE, SLOTS), 1).astype(F32)
    return (iota == column).astype(F32)


def band_slots(band):
    return jnp.concatenate(
        [
            band[row * CHAN : (row + 1) * CHAN, half * TILE : (half + 1) * TILE]
            for row in range(2)
            for half in range(2)
        ],
        axis=0,
    )


def slots_band(slots):
    return jnp.concatenate(
        [
            jnp.concatenate(
                [slots[(2 * row + half) * CHAN : (2 * row + half + 1) * CHAN] for half in range(2)],
                axis=1,
            )
            for row in range(2)
        ],
        axis=0,
    )


def gate_kernel(b0, b1, b2, b3, w_in, bias, gate, field, taps):
    me = lax.axis_index("lat")
    for shift, block in enumerate((b0, b1, b2, b3)):
        field[me ^ shift] = block[0].astype(F32)
    clear_taps(taps)

    def emit(row, value):
        squashed = jnp.tanh(value + bias[...])
        gate[row] = (1.0 - squashed * squashed).astype(BF16)

    conv_rows(field, w_in, taps, emit)


def rhs_kernel(
    counts, y0, y1, y2, y3, later, b0, b1, b2, b3, gate, w_in, w_out, out, out_b, field, taps, hidden
):
    me = lax.axis_index("lat")
    more = lax.axis_index("tm") < lax.axis_size("tm") - 1
    for shift, block in enumerate((b0, b1, b2, b3)):
        weights, slot, high, low = obs_of(block[1])
        hot = one_hot_t(slot)
        both = jnp.concatenate([hot * high, hot * low], axis=1).astype(BF16)
        slots = jnp.dot(
            both, jnp.concatenate([weights, weights], axis=0), preferred_element_type=F32
        )
        next_y = jnp.where(more, later[shift].astype(F32), 0.0)
        field[me ^ shift] = slots_band(slots) - next_y
    model_steps(field, gate, w_in, w_out, taps, hidden, counts[0])
    for shift, block in enumerate((y0, y1, y2, y3)):
        total = field[me ^ shift] + block[...].astype(F32)
        out[me ^ shift] = total
        out_b[me ^ shift] = total.astype(BF16)


def forward_kernel(counts, start, gate, w_in, w_out, out, out_b, taps, hidden):
    out[...] = start[...]
    model_steps(out, gate, w_in, w_out, taps, hidden, counts[0])
    out_b[...] = out[...].astype(BF16)


def observe_kernel(z, b0, b1, b2, b3, out):
    me = lax.axis_index("lat")
    for shift, block in enumerate((b0, b1, b2, b3)):
        weights, slot, _, _ = obs_of(block[1])
        weights = weights.astype(F32)
        high, low = split_16(band_slots(z[me ^ shift]))
        both = jnp.concatenate([high, low], axis=1)
        picked = jnp.dot(one_hot(slot).astype(BF16), both, preferred_element_type=F32)
        picked = picked[:, :TILE] + picked[:, TILE:]
        scaled = jnp.sum(picked * weights, axis=1, keepdims=True)
        high, low = split_16(weights * scaled)
        both = jnp.concatenate([high, low], axis=1)
        slots = jnp.dot(one_hot_t(slot).astype(BF16), both, preferred_element_type=F32)
        out[me ^ shift] = slots_band(slots[:, :TILE] + slots[:, TILE:])


def adjoint_kernel(
    counts, observed, z, later, precision, gate, w_in, w_out, out, taps, hidden
):
    me = lax.axis_index("lat")
    more = lax.axis_index("tm") < lax.axis_size("tm") - 1
    for shift in range(BANDS):
        at = me ^ shift
        weight = jnp.where(more, precision[shift].astype(F32), 0.0)
        out[at] = observed[at] - weight * (later[at].astype(F32) - z[at])
    model_steps(out, gate, w_in, w_out, taps, hidden, counts[0])


def image_of(at, tm_first, block, start, earlier, adjoint):
    before = jnp.where(tm_first, 0.0, earlier[at].astype(F32))
    return block[...].astype(F32) * (start[at] - before) + adjoint[at]


def image_kernel(start, earlier, adjoint, p0, p1, p2, p3, out, out_b):
    me = lax.axis_index("lat")
    tm_first = lax.axis_index("tm") == 0
    for shift, block in enumerate((p0, p1, p2, p3)):
        at = me ^ shift
        total = image_of(at, tm_first, block, start, earlier, adjoint)
        out[at] = total
        out_b[at] = total.astype(BF16)


def last_image_kernel(first, start, earlier, adjoint, p0, p1, p2, p3, own, dots):
    me = lax.axis_index("lat")
    tm_first = lax.axis_index("tm") == 0
    sums = [None] * 5
    for shift, block in enumerate((p0, p1, p2, p3)):
        at = me ^ shift
        total = image_of(at, tm_first, block, start, earlier, adjoint)
        if shift == 0:
            own[...] = total
        r0, v1 = first[at], start[at]
        for j, (a, b) in enumerate(((r0, r0), (r0, v1), (v1, v1), (r0, total), (v1, total))):
            piece = jnp.sum(a * b, axis=0, keepdims=True)
            sums[j] = piece if sums[j] is None else sums[j] + piece
    for j in range(5):
        value = jnp.sum(sums[j], axis=1, keepdims=True)
        dots[j : j + 1, :] = jnp.broadcast_to(value, (1, TILE))
    dots[5:8, :] = jnp.zeros((3, TILE), F32)


def finish_kernel(d0, d1, d2, d3, first, second, third, inc, res):
    me = lax.axis_index("lat")
    chan, _, lon = inc.shape
    total = (d0[...] + d1[...]) + (d2[...] + d3[...])
    rr0, c0, g11, g02, g12 = [total[j : j + 1, :1] for j in range(5)]
    a0 = rr0 / c0
    rr1 = rr0 - 2.0 * a0 * c0 + a0 * a0 * g11
    beta = rr1 / rr0
    grow = 1.0 + beta
    c1 = grow * grow * c0 - grow * a0 * (g02 + g11) + a0 * a0 * g12
    a1 = rr1 / c1
    wide = lambda value: jnp.broadcast_to(value, (chan, lon))
    inc_r, cross, twice = wide(a0 + a1 * grow), wide(a1 * a0), wide(a0 + a1 * grow)
    for row in range(2):
        at = row * CHAN
        r0 = first[me, at : at + chan, :]
        v1 = second[me, at : at + chan, :]
        v2 = third[at : at + chan, :]
        inc[:, row, :] = inc_r * r0 - cross * v1
        res[:, row, :] = r0 - twice * v1 + cross * v2


VMEM = pl.BlockSpec(memory_space=pltpu.VMEM)
SMEM = pl.BlockSpec(memory_space=pltpu.SMEM)


def call(kernel, name, ins, outs, scratch=(), scalars=0):
    specs = [SMEM] * scalars + [VMEM] * (len(ins) - scalars)
    return pl.pallas_call(
        kernel,
        name=name,
        out_shape=outs,
        in_specs=specs,
        out_specs=[VMEM] * len(outs),
        scratch_shapes=list(scratch),
        compiler_params=pltpu.CompilerParams(vmem_limit_bytes=48 << 20),
        cost_estimate=pl.CostEstimate(flops=1, bytes_accessed=1, transcendentals=0),
    )(*ins)


def stack_in(kernel):
    rows, cols, out_c, in_c = kernel.shape
    padded = jnp.pad(kernel, ((0, 0), (0, 0), (0, 0), (0, CHAN_IN - in_c)))
    block = jnp.transpose(padded, (2, 0, 1, 3)).reshape(out_c, rows, cols * CHAN_IN)
    block = jnp.pad(block, ((0, 0), (0, 0), (0, TAPS - cols * CHAN_IN)))
    return block.reshape(out_c, rows * TAPS)


def stack_out(kernel):
    rows, cols, out_c, in_c = kernel.shape
    padded = jnp.pad(kernel, ((0, 0), (0, 0), (0, CHAN - out_c), (0, 0)))
    none = jnp.zeros_like(padded[0])
    tap = lambda row_off: padded[row_off] if 0 <= row_off < rows else none
    blocks = [jnp.concatenate([tap(t - m) for t in range(4)], axis=-1) for m in range(2)]
    return jnp.concatenate(blocks, axis=0).reshape(2 * cols * CHAN, 4 * in_c)


def as_band(cells):
    rows, chan, lon = cells.shape
    return jnp.pad(cells.astype(BF16), ((0, 0), (0, CHAN - chan), (0, 0))).reshape(PAIR, lon)


def swap(block, shift):
    count = lax.axis_size("lat")
    return lax.ppermute(block, "lat", [(i, i ^ shift) for i in range(count)])


def by_partner(value):
    far = swap(value, 2)
    return [value, swap(value, 1), far, swap(far, 1)]


def along_tm(value, step):
    count = lax.axis_size("tm")
    return lax.ppermute(value, "tm", [(i, (i + step) % count) for i in range(count)])


def row_plan(
    departures,
    error_precision,
    trajectory,
    conv_in,
    conv_out,
    hidden_bias,
    step_counts,
    obs_tiles,
    obs_weights,
    innovations,
    obs_precision,
):
    _, rows, chan, lon = departures.shape
    hid = conv_in.shape[2]
    shape = lambda *dims: jax.ShapeDtypeStruct(dims, F32)
    shape_b = lambda *dims: jax.ShapeDtypeStruct(dims, BF16)
    whole, whole_b = shape(BANDS, PAIR, lon), shape_b(BANDS, PAIR, lon)

    root = jnp.sqrt(obs_precision[0])
    tiles = obs_tiles[0]
    per_row = 2 * chan
    slot = (2 * (tiles // per_row) + tiles % 2) * CHAN + (tiles // 2) % chan
    innov_high, innov_low = split_16(root * innovations[0])
    table = lambda value: value.astype(BF16).reshape(1, 2 * TILE)
    weights = (obs_weights[0] * root[:, None]).astype(BF16)
    obs_own = jnp.concatenate(
        [
            jnp.concatenate([weights[:TILE], weights[TILE:]], axis=1),
            table(slot // 2),
            table(slot % 2),
            table(innov_high),
            table(innov_low),
            jnp.zeros((OBS_ROWS - TILE - 4, 2 * TILE), BF16),
        ],
        axis=0,
    )
    both_own = jnp.stack([as_band(trajectory[0]), obs_own])
    prec_own = as_band(error_precision[0])

    y_all = by_partner(as_band(error_precision[0] * departures[0]))
    b_all = by_partner(both_own)
    p_all = by_partner(prec_own)
    y_later = along_tm(jnp.stack(y_all), -1)
    p_later = along_tm(jnp.stack(p_all), -1)

    fore_in, fore_out = stack_in(conv_in), stack_out(conv_out)
    back_in, back_out = stack_in(flipped(conv_out)), stack_out(flipped(conv_in))
    taps = pltpu.VMEM((ROWS, TAPS, lon), BF16)
    hidden = pltpu.VMEM((ROWS + 2, hid, lon), BF16)
    field = pltpu.VMEM((BANDS, PAIR, lon), F32)

    (gate,) = call(
        gate_kernel,
        "gate",
        (*b_all, fore_in, hidden_bias[:, None]),
        [shape_b(ROWS, hid, lon)],
        [field, taps],
    )
    r0, r0_b = call(
        rhs_kernel,
        "rhs",
        (step_counts, *y_all, y_later, *b_all, gate, back_in, back_out),
        [whole, whole_b],
        [field, taps, hidden],
        1,
    )

    def half(start, start_b):
        later = along_tm(start_b, -1)
        z, z_b = call(
            forward_kernel,
            "forward",
            (step_counts, start, gate, fore_in, fore_out),
            [whole, whole_b],
            [taps, hidden],
            1,
        )
        earlier = along_tm(z_b, 1)
        (observed,) = call(observe_kernel, "observe", (z, *b_all), [whole])
        (adjoint,) = call(
            adjoint_kernel,
            "adjoint",
            (step_counts, observed, z, later, p_later, gate, back_in, back_out),
            [whole],
            [taps, hidden],
            1,
        )
        return earlier, adjoint

    earlier, adjoint = half(r0, r0_b)
    v1, v1_b = call(image_kernel, "image", (r0, earlier, adjoint, *p_all), [whole, whole_b])
    earlier, adjoint = half(v1, v1_b)
    own, dots = call(
        last_image_kernel,
        "last_image",
        (r0, v1, earlier, adjoint, *p_all),
        [shape(PAIR, lon), shape(8, TILE)],
    )
    count = lax.axis_size("tm")
    parts = [dots] + [
        lax.ppermute(dots, "tm", [(i, i ^ step) for i in range(count)]) for step in range(1, count)
    ]
    inc, res = call(
        finish_kernel, "finish", (*parts, r0, v1, own), [shape(chan, rows, lon)] * 2
    )
    return (jnp.transpose(inc, (1, 0, 2))[None], jnp.transpose(res, (1, 0, 2))[None])


def solution(mesh):
    in_specs = (
        P(("ens", "tm"), "lat", None, None),
        P(("ens", "tm"), "lat", None, None),
        P(("ens", "tm"), "lat", None, None),
        P(),
        P(),
        P(),
        P(("ens", "tm")),
        P(("ens", "tm"), "lat"),
        P(("ens", "tm"), "lat", None),
        P(("ens", "tm"), "lat"),
        P(("ens", "tm"), "lat"),
    )
    out_specs = (P(("ens", "tm"), "lat", None, None), P(("ens", "tm"), "lat", None, None))
    plan = row_plan if mesh.shape["lat"] == BANDS and mesh.shape["tm"] == 4 else halo_plan
    return jax.shard_map(plan, mesh=mesh, in_specs=in_specs, out_specs=out_specs, check_vma=False)
```

```python
import functools

import jax
import jax.numpy as jnp
from jax import lax
from jax.experimental import pallas as pl
from jax.experimental.pallas import tpu as pltpu
from jax.sharding import PartitionSpec as P

TILE = 128
STEPS = 2
ITERS = 2
F32 = jnp.float32
BF16 = jnp.bfloat16


def padded_2(cells, sides, width):
    for axis, dim in sides:
        count = lax.axis_size(axis)
        ends = count - 1
        head = lax.slice_in_dim(cells, 0, width, axis=dim)
        tail = lax.slice_in_dim(cells, cells.shape[dim] - width, cells.shape[dim], axis=dim)
        cells = jnp.concatenate(
            [
                lax.ppermute(tail, axis, [(i, (i + 1) % count) for i in range(ends)]),
                cells,
                lax.ppermute(head, axis, [((i + 1) % count, i) for i in range(ends)]),
            ],
            axis=dim,
        )
    return cells


def from_behind(value, axis, steps):
    count = lax.axis_size(axis)
    leading, last = (max(0, -steps), min(count, count - steps))
    return lax.ppermute(value, axis, [(source, source + steps) for source in range(leading, last)])


def convolve_padded(padded, kernel):
    out_rows = padded.shape[0] - 2
    lon_len = padded.shape[2]
    wrapped = jnp.concatenate([padded[:, :, -1:], padded, padded[:, :, :1]], axis=2)
    accumulated = None
    for row_off in range(3):
        for col_off in range(3):
            window = wrapped[row_off : row_off + out_rows, :, col_off : col_off + lon_len]
            term = jnp.einsum(
                "oi,ril->rol", kernel[row_off, col_off], window, preferred_element_type=F32
            )
            accumulated = term if accumulated is None else accumulated + term
    return accumulated


def flipped(kernel):
    return jnp.transpose(kernel[::-1, ::-1], (0, 1, 3, 2))


def rim_wide(source):
    return padded_2(source, (("lat", 0),), 2)


def shift_up(source):
    return from_behind(source.astype(BF16), "tm", -1).astype(source.dtype)


def global_squares(source):
    return lax.psum(jnp.sum(source * source), ("tm", "lat"))


def halo_plan(
    departures,
    error_precision,
    trajectory,
    conv_in,
    conv_out,
    hidden_bias,
    step_counts,
    obs_tiles,
    obs_weights,
    innovations,
    obs_precision,
):
    precision = error_precision[0]
    own_count = step_counts[0]
    tile_index = obs_tiles[0]
    weights = obs_weights[0]
    innovation = innovations[0]
    obs_scale = obs_precision[0]
    back_in = flipped(conv_in)
    back_out = flipped(conv_out)
    trajectory_ext = padded_2(trajectory[0], (("lat", 0),), 1)
    gate_factor = (
        1.0 - jnp.tanh(convolve_padded(trajectory_ext, conv_in) + hidden_bias[:, None]) ** 2
    ).astype(BF16)
    gate_wide = padded_2(gate_factor, (("lat", 0),), 1)

    def one_step(current, first_kernel, second_kernel):
        widened = rim_wide(current.astype(BF16))
        hidden = (gate_wide.astype(F32) * convolve_padded(widened, first_kernel)).astype(BF16)
        return current + convolve_padded(hidden, second_kernel)

    def model(current, first_kernel, second_kernel):
        for step_index in range(STEPS):
            current = jnp.where(
                step_index < own_count, one_step(current, first_kernel, second_kernel), current
            )
        return current

    def observe_adjoint(scaled, like):
        tile_table = (
            jnp.zeros((like.size // TILE, TILE), F32)
            .at[tile_index]
            .add(weights * scaled[:, None])
        )
        return tile_table.reshape(like.shape)

    first_weighted = precision * departures[0]
    rhs = first_weighted + model(
        observe_adjoint(obs_scale * innovation, first_weighted) - shift_up(first_weighted),
        back_out,
        back_in,
    )
    increment = jnp.zeros_like(rhs)
    residual = rhs
    direction = rhs
    norm_now = global_squares(residual)
    for _ in range(ITERS):
        propagated = model(direction, conv_in, conv_out)
        earlier = from_behind(propagated.astype(BF16), "tm", 1).astype(F32)
        weighted = precision * (direction - earlier)
        picked = propagated.reshape(-1, TILE)[tile_index]
        observed = jnp.sum(picked * weights, axis=1)
        operator_image = weighted + model(
            observe_adjoint(obs_scale * observed, direction) - shift_up(weighted),
            back_out,
            back_in,
        )
        curvature = lax.psum(jnp.sum(direction * operator_image), ("tm", "lat"))
        step_length = norm_now / curvature
        increment = increment + step_length * direction
        residual = residual - step_length * operator_image
        norm_next = global_squares(residual)
        direction = residual + norm_next / norm_now * direction
        norm_now = norm_next
    return (increment[None], residual[None])


BANDS = 4
ROWS = 2 * BANDS
CHAN = 72
CHAN_IN = 80
TAPS = 256
PAIR = 2 * CHAN
SLOTS = 4 * CHAN
OBS_ROWS = 144


def row_of(ref, row):
    return ref[row // 2, (row % 2) * CHAN : (row % 2 + 1) * CHAN, :]


def taps_of(row):
    zeros = jnp.zeros((CHAN_IN - CHAN, row.shape[1]), F32)
    right = pltpu.roll(row, 1, axis=1)
    left = pltpu.roll(row, row.shape[1] - 1, axis=1)
    return jnp.concatenate([right, zeros, row, zeros, left, zeros], axis=0).astype(BF16)


def clear_taps(taps):
    used = 3 * CHAN_IN
    taps[:, used:, :] = jnp.zeros((ROWS, TAPS - used, taps.shape[2]), BF16)


def conv_rows(field, w_in, taps, emit):
    for row in range(ROWS):
        taps[row, : 3 * CHAN_IN] = taps_of(row_of(field, row))
    for row in range(ROWS):
        low, high = max(row - 1, 0), min(row + 2, ROWS)
        stacked = taps[low:high].reshape((high - low) * TAPS, taps.shape[2])
        skip = (low - (row - 1)) * TAPS
        weights = w_in[:, skip : skip + (high - low) * TAPS]
        emit(row, jnp.dot(weights, stacked, preferred_element_type=F32))


def model_steps(field, gate, w_in, w_out, taps, hidden, count):
    clear_taps(taps)
    hidden[0] = jnp.zeros(hidden.shape[1:], BF16)
    hidden[ROWS + 1] = jnp.zeros(hidden.shape[1:], BF16)

    def gated(row, value):
        hidden[row + 1] = (gate[row].astype(F32) * value).astype(BF16)

    def one_step(_, carry):
        conv_rows(field, w_in, taps, gated)
        for pair in range(BANDS):
            stacked = hidden[2 * pair : 2 * pair + 4].reshape(-1, hidden.shape[2])
            part = jnp.dot(w_out[...], stacked, preferred_element_type=F32)
            lon = part.shape[1]
            for row in range(2):
                tap = [part[(3 * row + b) * CHAN : (3 * row + b + 1) * CHAN] for b in range(3)]
                spread = pltpu.roll(tap[0], 1, axis=1) + tap[1] + pltpu.roll(tap[2], lon - 1, axis=1)
                at = row * CHAN
                field[pair, at : at + CHAN, :] = field[pair, at : at + CHAN, :] + spread
        return carry

    lax.fori_loop(0, jnp.minimum(count, STEPS), one_step, 0)


def split_16(value):
    high = value.astype(BF16)
    low = (value - high.astype(F32)).astype(BF16)
    return high, low


def obs_of(obs):
    weights = jnp.concatenate([obs[:TILE, :TILE], obs[:TILE, TILE:]], axis=0)
    extra = obs[TILE:, :].astype(F32)
    return weights, 2.0 * extra[0:1] + extra[1:2], extra[2:3], extra[3:4]


def one_hot_t(slot):
    iota = lax.broadcasted_iota(jnp.int32, (SLOTS, 2 * TILE), 0).astype(F32)
    return (iota == slot).astype(F32)


def one_hot(slot):
    columns = [
        jnp.transpose(jnp.broadcast_to(slot[:, half * TILE : (half + 1) * TILE], (TILE, TILE)))[:, :1]
        for half in range(2)
    ]
    column = jnp.concatenate(columns, axis=0)
    iota = lax.broadcasted_iota(jnp.int32, (2 * TILE, SLOTS), 1).astype(F32)
    return (iota == column).astype(F32)


def band_slots(band):
    return jnp.concatenate(
        [
            band[row * CHAN : (row + 1) * CHAN, half * TILE : (half + 1) * TILE]
            for row in range(2)
            for half in range(2)
        ],
        axis=0,
    )


def slots_band(slots):
    return jnp.concatenate(
        [
            jnp.concatenate(
                [slots[(2 * row + half) * CHAN : (2 * row + half + 1) * CHAN] for half in range(2)],
                axis=1,
            )
            for row in range(2)
        ],
        axis=0,
    )


def gate_kernel(b0, b1, b2, b3, w_in, bias, gate, field, taps):
    me = lax.axis_index("lat")
    for shift, block in enumerate((b0, b1, b2, b3)):
        field[me ^ shift] = block[0].astype(F32)
    clear_taps(taps)

    def emit(row, value):
        squashed = jnp.tanh(value + bias[...])
        gate[row] = (1.0 - squashed * squashed).astype(BF16)

    conv_rows(field, w_in, taps, emit)


def rhs_kernel(
    counts, y0, y1, y2, y3, later, b0, b1, b2, b3, gate, w_in, w_out, out, out_b, field, taps, hidden
):
    me = lax.axis_index("lat")
    more = lax.axis_index("tm") < lax.axis_size("tm") - 1
    for shift, block in enumerate((b0, b1, b2, b3)):
        weights, slot, high, low = obs_of(block[1])
        hot = one_hot_t(slot)
        both = jnp.concatenate([hot * high, hot * low], axis=1).astype(BF16)
        slots = jnp.dot(
            both, jnp.concatenate([weights, weights], axis=0), preferred_element_type=F32
        )
        next_y = jnp.where(more, later[shift].astype(F32), 0.0)
        field[me ^ shift] = slots_band(slots) - next_y
    model_steps(field, gate, w_in, w_out, taps, hidden, counts[0])
    for shift, block in enumerate((y0, y1, y2, y3)):
        total = field[me ^ shift] + block[...].astype(F32)
        out[me ^ shift] = total
        out_b[me ^ shift] = total.astype(BF16)


def forward_kernel(counts, start, gate, w_in, w_out, out, out_b, taps, hidden):
    out[...] = start[...]
    model_steps(out, gate, w_in, w_out, taps, hidden, counts[0])
    out_b[...] = out[...].astype(BF16)


def observe_kernel(z, b0, b1, b2, b3, out, energy):
    me = lax.axis_index("lat")
    squares = jnp.zeros((1, 1), F32)
    for shift, block in enumerate((b0, b1, b2, b3)):
        weights, slot, _, _ = obs_of(block[1])
        weights = weights.astype(F32)
        high, low = split_16(band_slots(z[me ^ shift]))
        both = jnp.concatenate([high, low], axis=1)
        picked = jnp.dot(one_hot(slot).astype(BF16), both, preferred_element_type=F32)
        picked = picked[:, :TILE] + picked[:, TILE:]
        scaled = jnp.sum(picked * weights, axis=1, keepdims=True)
        squares = squares + jnp.sum(scaled * scaled, axis=0, keepdims=True)
        high, low = split_16(weights * scaled)
        both = jnp.concatenate([high, low], axis=1)
        slots = jnp.dot(one_hot_t(slot).astype(BF16), both, preferred_element_type=F32)
        out[me ^ shift] = slots_band(slots[:, :TILE] + slots[:, TILE:])
    energy[...] = jnp.broadcast_to(squares, energy.shape)


def adjoint_kernel(
    counts, observed, z, later, precision, gate, w_in, w_out, out, taps, hidden
):
    me = lax.axis_index("lat")
    more = lax.axis_index("tm") < lax.axis_size("tm") - 1
    for shift in range(BANDS):
        at = me ^ shift
        weight = jnp.where(more, precision[shift].astype(F32), 0.0)
        out[at] = observed[at] - weight * (later[at].astype(F32) - z[at])
    model_steps(out, gate, w_in, w_out, taps, hidden, counts[0])


def image_of(at, tm_first, block, start, earlier, adjoint):
    before = jnp.where(tm_first, 0.0, earlier[at].astype(F32))
    return block.astype(F32) * (start[at] - before) + adjoint[at]


def image_kernel(start, earlier, adjoint, p0, p1, p2, p3, out, out_b):
    me = lax.axis_index("lat")
    tm_first = lax.axis_index("tm") == 0
    for shift, block in enumerate((p0, p1, p2, p3)):
        at = me ^ shift
        total = image_of(at, tm_first, block[...], start, earlier, adjoint)
        out[at] = total
        out_b[at] = total.astype(BF16)


def products_kernel(first, second, z, later, precision, p0, p1, p2, p3, energy, dots):
    me = lax.axis_index("lat")
    tm_first = lax.axis_index("tm") == 0
    more = lax.axis_index("tm") < lax.axis_size("tm") - 1
    sums = [jnp.zeros((1, first.shape[2]), F32) for _ in range(4)]
    for shift, block in enumerate((p0, p1, p2, p3)):
        at = me ^ shift
        r0, v1 = first[at], second[at]
        misfit = later[at].astype(F32) - z[at]
        weight = jnp.where(more, precision[shift].astype(F32), 0.0)
        initial = jnp.where(tm_first, block[...].astype(F32), 0.0)
        terms = (r0 * r0, r0 * v1, v1 * v1, weight * misfit * misfit + initial * v1 * v1)
        sums = [total + jnp.sum(term, axis=0, keepdims=True) for total, term in zip(sums, terms)]
    for j, total in enumerate(sums):
        value = jnp.broadcast_to(jnp.sum(total, axis=1, keepdims=True), (1, TILE))
        dots[j : j + 1, :] = value + energy[:1, :] if j == 3 else value
    dots[4:8, :] = jnp.zeros((4, TILE), F32)


def finish_kernel(d0, d1, d2, d3, first, second, earlier, adjoint, p0, inc, res):
    me = lax.axis_index("lat")
    tm_first = lax.axis_index("tm") == 0
    chan, _, lon = inc.shape
    total = (d0[...] + d1[...]) + (d2[...] + d3[...])
    rr0, c0, g11, g12 = [total[j : j + 1, :1] for j in range(4)]
    a0 = rr0 / c0
    rr1 = rr0 - 2.0 * a0 * c0 + a0 * a0 * g11
    beta = rr1 / rr0
    grow = 1.0 + beta
    c1 = grow * grow * c0 - 2.0 * grow * a0 * g11 + a0 * a0 * g12
    a1 = rr1 / c1
    wide = lambda value: jnp.broadcast_to(value, (chan, lon))
    along, cross = wide(a0 + a1 * grow), wide(a1 * a0)
    image = image_of(me, tm_first, p0[...], second, earlier, adjoint)
    r0_own, v1_own = first[me], second[me]
    for row in range(2):
        at = row * CHAN
        r0, v1, v2 = [field[at : at + chan] for field in (r0_own, v1_own, image)]
        inc[:, row, :] = along * r0 - cross * v1
        res[:, row, :] = r0 - along * v1 + cross * v2


VMEM = pl.BlockSpec(memory_space=pltpu.VMEM)
SMEM = pl.BlockSpec(memory_space=pltpu.SMEM)


def call(kernel, name, ins, outs, scratch=(), scalars=0):
    specs = [SMEM] * scalars + [VMEM] * (len(ins) - scalars)
    return pl.pallas_call(
        kernel,
        name=name,
        out_shape=outs,
        in_specs=specs,
        out_specs=[VMEM] * len(outs),
        scratch_shapes=list(scratch),
        compiler_params=pltpu.CompilerParams(vmem_limit_bytes=48 << 20),
        cost_estimate=pl.CostEstimate(flops=1, bytes_accessed=1, transcendentals=0),
    )(*ins)


def stack_in(kernel):
    rows, cols, out_c, in_c = kernel.shape
    padded = jnp.pad(kernel, ((0, 0), (0, 0), (0, 0), (0, CHAN_IN - in_c)))
    block = jnp.transpose(padded, (2, 0, 1, 3)).reshape(out_c, rows, cols * CHAN_IN)
    block = jnp.pad(block, ((0, 0), (0, 0), (0, TAPS - cols * CHAN_IN)))
    return block.reshape(out_c, rows * TAPS)


def stack_out(kernel):
    rows, cols, out_c, in_c = kernel.shape
    padded = jnp.pad(kernel, ((0, 0), (0, 0), (0, CHAN - out_c), (0, 0)))
    none = jnp.zeros_like(padded[0])
    tap = lambda row_off: padded[row_off] if 0 <= row_off < rows else none
    blocks = [jnp.concatenate([tap(t - m) for t in range(4)], axis=-1) for m in range(2)]
    return jnp.concatenate(blocks, axis=0).reshape(2 * cols * CHAN, 4 * in_c)


def as_band(cells):
    rows, chan, lon = cells.shape
    return jnp.pad(cells.astype(BF16), ((0, 0), (0, CHAN - chan), (0, 0))).reshape(PAIR, lon)


def swap(block, shift):
    count = lax.axis_size("lat")
    return lax.ppermute(block, "lat", [(i, i ^ shift) for i in range(count)])


def by_partner(value):
    far = swap(value, 2)
    return [value, swap(value, 1), far, swap(far, 1)]


def along_tm(value, step):
    count = lax.axis_size("tm")
    return lax.ppermute(value, "tm", [(i, (i + step) % count) for i in range(count)])


def row_plan(
    departures,
    error_precision,
    trajectory,
    conv_in,
    conv_out,
    hidden_bias,
    step_counts,
    obs_tiles,
    obs_weights,
    innovations,
    obs_precision,
):
    _, rows, chan, lon = departures.shape
    hid = conv_in.shape[2]
    shape = lambda *dims: jax.ShapeDtypeStruct(dims, F32)
    shape_b = lambda *dims: jax.ShapeDtypeStruct(dims, BF16)
    whole, whole_b = shape(BANDS, PAIR, lon), shape_b(BANDS, PAIR, lon)

    root = jnp.sqrt(obs_precision[0])
    tiles = obs_tiles[0]
    per_row = 2 * chan
    slot = (2 * (tiles // per_row) + tiles % 2) * CHAN + (tiles // 2) % chan
    innov_high, innov_low = split_16(root * innovations[0])
    table = lambda value: value.astype(BF16).reshape(1, 2 * TILE)
    weights = (obs_weights[0] * root[:, None]).astype(BF16)
    obs_own = jnp.concatenate(
        [
            jnp.concatenate([weights[:TILE], weights[TILE:]], axis=1),
            table(slot // 2),
            table(slot % 2),
            table(innov_high),
            table(innov_low),
            jnp.zeros((OBS_ROWS - TILE - 4, 2 * TILE), BF16),
        ],
        axis=0,
    )
    both_own = jnp.stack([as_band(trajectory[0]), obs_own])
    prec_own = as_band(error_precision[0])

    y_all = by_partner(as_band(error_precision[0] * departures[0]))
    b_all = by_partner(both_own)
    p_all = by_partner(prec_own)
    y_later = along_tm(jnp.stack(y_all), -1)
    p_later = along_tm(jnp.stack(p_all), -1)

    fore_in, fore_out = stack_in(conv_in), stack_out(conv_out)
    back_in, back_out = stack_in(flipped(conv_out)), stack_out(flipped(conv_in))
    taps = pltpu.VMEM((ROWS, TAPS, lon), BF16)
    hidden = pltpu.VMEM((ROWS + 2, hid, lon), BF16)
    field = pltpu.VMEM((BANDS, PAIR, lon), F32)

    (gate,) = call(
        gate_kernel,
        "gate",
        (*b_all, fore_in, hidden_bias[:, None]),
        [shape_b(ROWS, hid, lon)],
        [field, taps],
    )
    r0, r0_b = call(
        rhs_kernel,
        "rhs",
        (step_counts, *y_all, y_later, *b_all, gate, back_in, back_out),
        [whole, whole_b],
        [field, taps, hidden],
        1,
    )

    def to_misfits(start, start_b):
        later = along_tm(start_b, -1)
        z, z_b = call(
            forward_kernel,
            "forward",
            (step_counts, start, gate, fore_in, fore_out),
            [whole, whole_b],
            [taps, hidden],
            1,
        )
        observed, energy = call(observe_kernel, "observe", (z, *b_all), [whole, shape(8, TILE)])
        return along_tm(z_b, 1), later, z, observed, energy

    def adjoint_of(later, z, observed):
        return call(
            adjoint_kernel,
            "adjoint",
            (step_counts, observed, z, later, p_later, gate, back_in, back_out),
            [whole],
            [taps, hidden],
            1,
        )[0]

    earlier, later, z, observed, _ = to_misfits(r0, r0_b)
    adjoint = adjoint_of(later, z, observed)
    v1, v1_b = call(image_kernel, "image", (r0, earlier, adjoint, *p_all), [whole, whole_b])
    earlier, later, z, observed, energy = to_misfits(v1, v1_b)
    (dots,) = call(
        products_kernel,
        "products",
        (r0, v1, z, later, p_later, *p_all, energy),
        [shape(8, TILE)],
    )
    count = lax.axis_size("tm")
    parts = [dots] + [
        lax.ppermute(dots, "tm", [(i, i ^ step) for i in range(count)]) for step in range(1, count)
    ]
    observed, _ = lax.optimization_barrier((observed, dots))
    adjoint = adjoint_of(later, z, observed)
    inc, res = call(
        finish_kernel,
        "finish",
        (*parts, r0, v1, earlier, adjoint, p_all[0]),
        [shape(chan, rows, lon)] * 2,
    )
    return (jnp.transpose(inc, (1, 0, 2))[None], jnp.transpose(res, (1, 0, 2))[None])


def solution(mesh):
    in_specs = (
        P(("ens", "tm"), "lat", None, None),
        P(("ens", "tm"), "lat", None, None),
        P(("ens", "tm"), "lat", None, None),
        P(),
        P(),
        P(),
        P(("ens", "tm")),
        P(("ens", "tm"), "lat"),
        P(("ens", "tm"), "lat", None),
        P(("ens", "tm"), "lat"),
        P(("ens", "tm"), "lat"),
    )
    out_specs = (P(("ens", "tm"), "lat", None, None), P(("ens", "tm"), "lat", None, None))
    plan = row_plan if mesh.shape["lat"] == BANDS and mesh.shape["tm"] == 4 else halo_plan
    return jax.shard_map(plan, mesh=mesh, in_specs=in_specs, out_specs=out_specs, check_vma=False)
```

```python
import functools

import jax
import jax.numpy as jnp
from jax import lax
from jax.experimental import pallas as pl
from jax.experimental.pallas import tpu as pltpu
from jax.sharding import PartitionSpec as P

TILE = 128
STEPS = 2
ITERS = 2
F32 = jnp.float32
BF16 = jnp.bfloat16


def padded_2(cells, sides, width):
    for axis, dim in sides:
        count = lax.axis_size(axis)
        ends = count - 1
        head = lax.slice_in_dim(cells, 0, width, axis=dim)
        tail = lax.slice_in_dim(cells, cells.shape[dim] - width, cells.shape[dim], axis=dim)
        cells = jnp.concatenate(
            [
                lax.ppermute(tail, axis, [(i, (i + 1) % count) for i in range(ends)]),
                cells,
                lax.ppermute(head, axis, [((i + 1) % count, i) for i in range(ends)]),
            ],
            axis=dim,
        )
    return cells


def from_behind(value, axis, steps):
    count = lax.axis_size(axis)
    leading, last = (max(0, -steps), min(count, count - steps))
    return lax.ppermute(value, axis, [(source, source + steps) for source in range(leading, last)])


def convolve_padded(padded, kernel):
    out_rows = padded.shape[0] - 2
    lon_len = padded.shape[2]
    wrapped = jnp.concatenate([padded[:, :, -1:], padded, padded[:, :, :1]], axis=2)
    accumulated = None
    for row_off in range(3):
        for col_off in range(3):
            window = wrapped[row_off : row_off + out_rows, :, col_off : col_off + lon_len]
            term = jnp.einsum(
                "oi,ril->rol", kernel[row_off, col_off], window, preferred_element_type=F32
            )
            accumulated = term if accumulated is None else accumulated + term
    return accumulated


def flipped(kernel):
    return jnp.transpose(kernel[::-1, ::-1], (0, 1, 3, 2))


def rim_wide(source):
    return padded_2(source, (("lat", 0),), 2)


def shift_up(source):
    return from_behind(source.astype(BF16), "tm", -1).astype(source.dtype)


def global_squares(source):
    return lax.psum(jnp.sum(source * source), ("tm", "lat"))


def halo_plan(
    departures,
    error_precision,
    trajectory,
    conv_in,
    conv_out,
    hidden_bias,
    step_counts,
    obs_tiles,
    obs_weights,
    innovations,
    obs_precision,
):
    precision = error_precision[0]
    own_count = step_counts[0]
    tile_index = obs_tiles[0]
    weights = obs_weights[0]
    innovation = innovations[0]
    obs_scale = obs_precision[0]
    back_in = flipped(conv_in)
    back_out = flipped(conv_out)
    trajectory_ext = padded_2(trajectory[0], (("lat", 0),), 1)
    gate_factor = (
        1.0 - jnp.tanh(convolve_padded(trajectory_ext, conv_in) + hidden_bias[:, None]) ** 2
    ).astype(BF16)
    gate_wide = padded_2(gate_factor, (("lat", 0),), 1)

    def one_step(current, first_kernel, second_kernel):
        widened = rim_wide(current.astype(BF16))
        hidden = (gate_wide.astype(F32) * convolve_padded(widened, first_kernel)).astype(BF16)
        return current + convolve_padded(hidden, second_kernel)

    def model(current, first_kernel, second_kernel):
        for step_index in range(STEPS):
            current = jnp.where(
                step_index < own_count, one_step(current, first_kernel, second_kernel), current
            )
        return current

    def observe_adjoint(scaled, like):
        tile_table = (
            jnp.zeros((like.size // TILE, TILE), F32)
            .at[tile_index]
            .add(weights * scaled[:, None])
        )
        return tile_table.reshape(like.shape)

    first_weighted = precision * departures[0]
    rhs = first_weighted + model(
        observe_adjoint(obs_scale * innovation, first_weighted) - shift_up(first_weighted),
        back_out,
        back_in,
    )
    increment = jnp.zeros_like(rhs)
    residual = rhs
    direction = rhs
    norm_now = global_squares(residual)
    for _ in range(ITERS):
        propagated = model(direction, conv_in, conv_out)
        earlier = from_behind(propagated.astype(BF16), "tm", 1).astype(F32)
        weighted = precision * (direction - earlier)
        picked = propagated.reshape(-1, TILE)[tile_index]
        observed = jnp.sum(picked * weights, axis=1)
        operator_image = weighted + model(
            observe_adjoint(obs_scale * observed, direction) - shift_up(weighted),
            back_out,
            back_in,
        )
        curvature = lax.psum(jnp.sum(direction * operator_image), ("tm", "lat"))
        step_length = norm_now / curvature
        increment = increment + step_length * direction
        residual = residual - step_length * operator_image
        norm_next = global_squares(residual)
        direction = residual + norm_next / norm_now * direction
        norm_now = norm_next
    return (increment[None], residual[None])


BANDS = 4
ROWS = 2 * BANDS
CHAN = 72
CHAN_IN = 80
TAPS = 256
PAIR = 2 * CHAN
SLOTS = 4 * CHAN
OBS_ROWS = 144


def row_of(ref, row):
    return ref[row // 2, (row % 2) * CHAN : (row % 2 + 1) * CHAN, :]


def taps_of(row):
    zeros = jnp.zeros((CHAN_IN - CHAN, row.shape[1]), F32)
    right = pltpu.roll(row, 1, axis=1)
    left = pltpu.roll(row, row.shape[1] - 1, axis=1)
    return jnp.concatenate([right, zeros, row, zeros, left, zeros], axis=0).astype(BF16)


def clear_taps(taps):
    used = 3 * CHAN_IN
    taps[:, used:, :] = jnp.zeros((ROWS, TAPS - used, taps.shape[2]), BF16)


def conv_rows(field, w_in, taps, emit):
    for row in range(ROWS):
        taps[row, : 3 * CHAN_IN] = taps_of(row_of(field, row))
    for row in range(ROWS):
        low, high = max(row - 1, 0), min(row + 2, ROWS)
        stacked = taps[low:high].reshape((high - low) * TAPS, taps.shape[2])
        skip = (low - (row - 1)) * TAPS
        weights = w_in[:, skip : skip + (high - low) * TAPS]
        emit(row, jnp.dot(weights, stacked, preferred_element_type=F32))


def prepare(taps, hidden):
    clear_taps(taps)
    hidden[0] = jnp.zeros(hidden.shape[1:], BF16)
    hidden[ROWS + 1] = jnp.zeros(hidden.shape[1:], BF16)


def model_step(source, target, target_b, gate, w_in, w_out, taps, hidden):
    def gated(row, value):
        hidden[row + 1] = (gate[row].astype(F32) * value).astype(BF16)

    conv_rows(source, w_in, taps, gated)
    for pair in range(BANDS):
        stacked = hidden[2 * pair : 2 * pair + 4].reshape(-1, hidden.shape[2])
        part = jnp.dot(w_out[...], stacked, preferred_element_type=F32)
        lon = part.shape[1]
        rows = []
        for row in range(2):
            tap = [part[(3 * row + b) * CHAN : (3 * row + b + 1) * CHAN] for b in range(3)]
            spread = pltpu.roll(tap[0], 1, axis=1) + tap[1] + pltpu.roll(tap[2], lon - 1, axis=1)
            rows.append(source[pair, row * CHAN : (row + 1) * CHAN, :] + spread)
        band = jnp.concatenate(rows, axis=0)
        target[pair] = band
        if target_b is not None:
            target_b[pair] = band.astype(BF16)


def model_steps(field, gate, w_in, w_out, taps, hidden, count):
    prepare(taps, hidden)

    def one_step(_, carry):
        model_step(field, field, None, gate, w_in, w_out, taps, hidden)
        return carry

    lax.fori_loop(0, jnp.minimum(count, STEPS), one_step, 0)


def forward_steps(start, out, out_b, gate, w_in, w_out, taps, hidden, count):
    prepare(taps, hidden)
    model_step(start, out, out_b, gate, w_in, w_out, taps, hidden)

    def one_step(_, carry):
        model_step(out, out, out_b, gate, w_in, w_out, taps, hidden)
        return carry

    lax.fori_loop(1, jnp.minimum(count, STEPS), one_step, 0)


def split_16(value):
    high = value.astype(BF16)
    low = (value - high.astype(F32)).astype(BF16)
    return high, low


def obs_of(obs):
    weights = jnp.concatenate([obs[:TILE, :TILE], obs[:TILE, TILE:]], axis=0)
    extra = obs[TILE:, :].astype(F32)
    return weights, 2.0 * extra[0:1] + extra[1:2], extra[2:3], extra[3:4]


def one_hot_t(slot):
    iota = lax.broadcasted_iota(jnp.int32, (SLOTS, 2 * TILE), 0).astype(F32)
    return (iota == slot).astype(F32)


def one_hot(slot):
    columns = [
        jnp.transpose(jnp.broadcast_to(slot[:, half * TILE : (half + 1) * TILE], (TILE, TILE)))[:, :1]
        for half in range(2)
    ]
    column = jnp.concatenate(columns, axis=0)
    iota = lax.broadcasted_iota(jnp.int32, (2 * TILE, SLOTS), 1).astype(F32)
    return (iota == column).astype(F32)


def band_slots(band):
    return jnp.concatenate(
        [
            band[row * CHAN : (row + 1) * CHAN, half * TILE : (half + 1) * TILE]
            for row in range(2)
            for half in range(2)
        ],
        axis=0,
    )


def slots_band(slots):
    return jnp.concatenate(
        [
            jnp.concatenate(
                [slots[(2 * row + half) * CHAN : (2 * row + half + 1) * CHAN] for half in range(2)],
                axis=1,
            )
            for row in range(2)
        ],
        axis=0,
    )


def rhs_kernel(
    counts,
    y0, y1, y2, y3,
    later,
    b0, b1, b2, b3,
    fore_in, bias, w_in, w_out,
    gate, out, out_b,
    field, taps, hidden,
):
    me = lax.axis_index("lat")
    more = lax.axis_index("tm") < lax.axis_size("tm") - 1
    blocks = (b0, b1, b2, b3)
    for shift, block in enumerate(blocks):
        field[me ^ shift] = block[0].astype(F32)
    prepare(taps, hidden)

    def emit(row, value):
        squashed = jnp.tanh(value + bias[...])
        gate[row] = (1.0 - squashed * squashed).astype(BF16)

    conv_rows(field, fore_in, taps, emit)
    for shift, block in enumerate(blocks):
        weights, slot, high, low = obs_of(block[1])
        hot = one_hot_t(slot)
        both = jnp.concatenate([hot * high, hot * low], axis=1).astype(BF16)
        slots = jnp.dot(
            both, jnp.concatenate([weights, weights], axis=0), preferred_element_type=F32
        )
        next_y = jnp.where(more, later[shift].astype(F32), 0.0)
        field[me ^ shift] = slots_band(slots) - next_y

    def one_step(_, carry):
        model_step(field, field, None, gate, w_in, w_out, taps, hidden)
        return carry

    lax.fori_loop(0, jnp.minimum(counts[0], STEPS), one_step, 0)
    for shift, block in enumerate((y0, y1, y2, y3)):
        total = field[me ^ shift] + block[...].astype(F32)
        out[me ^ shift] = total
        out_b[me ^ shift] = total.astype(BF16)


def forward_kernel(counts, start, gate, w_in, w_out, out, out_b, taps, hidden):
    forward_steps(start, out, out_b, gate, w_in, w_out, taps, hidden, counts[0])


def observed_band(z_band, pick, spread, weights):
    ones = jnp.ones((2 * TILE, TILE), BF16)

    def product(left, value):
        return jnp.dot(left, jnp.concatenate(split_16(value), axis=1), preferred_element_type=F32)

    picked = product(pick, band_slots(z_band))
    terms = (picked[:, :TILE] + picked[:, TILE:]) * weights
    terms = jnp.concatenate(split_16(terms), axis=1)
    scaled = jnp.dot(terms, ones, preferred_element_type=F32)
    slots = product(spread, weights * scaled)
    squares = jnp.sum(scaled * scaled, axis=0, keepdims=True)
    return slots_band(slots[:, :TILE] + slots[:, TILE:]), squares


def observe_kernel(z, b0, b1, b2, b3, out, pick, spread, weights):
    me = lax.axis_index("lat")
    for shift, block in enumerate((b0, b1, b2, b3)):
        at = me ^ shift
        own, slot, _, _ = obs_of(block[1])
        pick[at] = one_hot(slot).astype(BF16)
        spread[at] = one_hot_t(slot).astype(BF16)
        weights[at] = own.astype(F32)
    for band in range(BANDS):
        out[band], _ = observed_band(z[band], pick[band], spread[band], weights[band])


def observe_again_kernel(z, pick, spread, weights, out, energy):
    squares = jnp.zeros((1, TILE), F32)
    for band in range(BANDS):
        out[band], own = observed_band(z[band], pick[band], spread[band], weights[band])
        squares = squares + own
    energy[...] = jnp.broadcast_to(squares, energy.shape)


def next_misfit(at, shift, later, z, precision):
    more = lax.axis_index("tm") < lax.axis_size("tm") - 1
    weight = jnp.where(more, precision[shift].astype(F32), 0.0)
    return later[at].astype(F32) - z[at], weight


def adjoint_kernel(
    counts, observed, z, later, precision, gate, w_in, w_out, field, taps, hidden
):
    me = lax.axis_index("lat")
    for shift in range(BANDS):
        at = me ^ shift
        misfit, weight = next_misfit(at, shift, later, z, precision)
        field[at] = observed[at] - weight * misfit
    model_steps(field, gate, w_in, w_out, taps, hidden, counts[0])


def image_of(at, block, start, earlier, adjoint):
    before = jnp.where(lax.axis_index("tm") == 0, 0.0, earlier[at].astype(F32))
    return block.astype(F32) * (start[at] - before) + adjoint[at]


def image_kernel(start, earlier, adjoint, p0, p1, p2, p3, out, out_b):
    me = lax.axis_index("lat")
    for shift, block in enumerate((p0, p1, p2, p3)):
        at = me ^ shift
        total = image_of(at, block[...], start, earlier, adjoint)
        out[at] = total
        out_b[at] = total.astype(BF16)


def products_kernel(first, second, z, later, precision, p0, p1, p2, p3, energy, dots):
    me = lax.axis_index("lat")
    tm_first = lax.axis_index("tm") == 0
    sums = [jnp.zeros((1, first.shape[2]), F32) for _ in range(4)]
    for shift, block in enumerate((p0, p1, p2, p3)):
        at = me ^ shift
        r0, v1 = first[at], second[at]
        misfit, weight = next_misfit(at, shift, later, z, precision)
        initial = jnp.where(tm_first, block[...].astype(F32), 0.0)
        terms = (r0 * r0, r0 * v1, v1 * v1, weight * misfit * misfit + initial * v1 * v1)
        sums = [total + jnp.sum(term, axis=0, keepdims=True) for total, term in zip(sums, terms)]
    for j, total in enumerate(sums):
        value = jnp.broadcast_to(jnp.sum(total, axis=1, keepdims=True), (1, TILE))
        dots[j : j + 1, :] = value + energy[:1, :] if j == 3 else value
    dots[4:8, :] = jnp.zeros((4, TILE), F32)


def finish_kernel(d0, d1, d2, d3, first, second, earlier, adjoint, p0, inc, res):
    me = lax.axis_index("lat")
    chan, _, lon = inc.shape
    total = (d0[...] + d1[...]) + (d2[...] + d3[...])
    rr0, c0, g11, g12 = [total[j : j + 1, :1] for j in range(4)]
    a0 = rr0 / c0
    rr1 = rr0 - 2.0 * a0 * c0 + a0 * a0 * g11
    beta = rr1 / rr0
    grow = 1.0 + beta
    c1 = grow * grow * c0 - 2.0 * grow * a0 * g11 + a0 * a0 * g12
    a1 = rr1 / c1
    wide = lambda value: jnp.broadcast_to(value, (chan, lon))
    along, cross = wide(a0 + a1 * grow), wide(a1 * a0)
    image = image_of(me, p0[...], second, earlier, adjoint)
    r0_own, v1_own = first[me], second[me]
    for row in range(2):
        at = row * CHAN
        r0, v1, v2 = [field[at : at + chan] for field in (r0_own, v1_own, image)]
        inc[:, row, :] = along * r0 - cross * v1
        res[:, row, :] = r0 - along * v1 + cross * v2


VMEM = pl.BlockSpec(memory_space=pltpu.VMEM)
SMEM = pl.BlockSpec(memory_space=pltpu.SMEM)


def call(kernel, name, ins, outs, scratch=(), scalars=0):
    specs = [SMEM] * scalars + [VMEM] * (len(ins) - scalars)
    return pl.pallas_call(
        kernel,
        name=name,
        out_shape=outs,
        in_specs=specs,
        out_specs=[VMEM] * len(outs),
        scratch_shapes=list(scratch),
        compiler_params=pltpu.CompilerParams(vmem_limit_bytes=48 << 20),
        cost_estimate=pl.CostEstimate(flops=1, bytes_accessed=1, transcendentals=0),
    )(*ins)


def stack_in(kernel):
    rows, cols, out_c, in_c = kernel.shape
    padded = jnp.pad(kernel, ((0, 0), (0, 0), (0, 0), (0, CHAN_IN - in_c)))
    block = jnp.transpose(padded, (2, 0, 1, 3)).reshape(out_c, rows, cols * CHAN_IN)
    block = jnp.pad(block, ((0, 0), (0, 0), (0, TAPS - cols * CHAN_IN)))
    return block.reshape(out_c, rows * TAPS)


def stack_out(kernel):
    rows, cols, out_c, in_c = kernel.shape
    padded = jnp.pad(kernel, ((0, 0), (0, 0), (0, CHAN - out_c), (0, 0)))
    none = jnp.zeros_like(padded[0])
    tap = lambda row_off: padded[row_off] if 0 <= row_off < rows else none
    blocks = [jnp.concatenate([tap(t - m) for t in range(4)], axis=-1) for m in range(2)]
    return jnp.concatenate(blocks, axis=0).reshape(2 * cols * CHAN, 4 * in_c)


def as_band(cells):
    rows, chan, lon = cells.shape
    return jnp.pad(cells.astype(BF16), ((0, 0), (0, CHAN - chan), (0, 0))).reshape(PAIR, lon)


def swap(block, shift):
    count = lax.axis_size("lat")
    return lax.ppermute(block, "lat", [(i, i ^ shift) for i in range(count)])


def by_partner(value):
    far = swap(value, 2)
    return [value, swap(value, 1), far, swap(far, 1)]


def along_tm(value, step):
    count = lax.axis_size("tm")
    return lax.ppermute(value, "tm", [(i, (i + step) % count) for i in range(count)])


def row_plan(
    departures,
    error_precision,
    trajectory,
    conv_in,
    conv_out,
    hidden_bias,
    step_counts,
    obs_tiles,
    obs_weights,
    innovations,
    obs_precision,
):
    _, rows, chan, lon = departures.shape
    hid = conv_in.shape[2]
    shape = lambda *dims: jax.ShapeDtypeStruct(dims, F32)
    shape_b = lambda *dims: jax.ShapeDtypeStruct(dims, BF16)
    whole, whole_b = shape(BANDS, PAIR, lon), shape_b(BANDS, PAIR, lon)

    root = jnp.sqrt(obs_precision[0])
    tiles = obs_tiles[0]
    per_row = 2 * chan
    slot = (2 * (tiles // per_row) + tiles % 2) * CHAN + (tiles // 2) % chan
    innov_high, innov_low = split_16(root * innovations[0])
    table = lambda value: value.astype(BF16).reshape(1, 2 * TILE)
    weights = (obs_weights[0] * root[:, None]).astype(BF16)
    obs_own = jnp.concatenate(
        [
            jnp.concatenate([weights[:TILE], weights[TILE:]], axis=1),
            table(slot // 2),
            table(slot % 2),
            table(innov_high),
            table(innov_low),
            jnp.zeros((OBS_ROWS - TILE - 4, 2 * TILE), BF16),
        ],
        axis=0,
    )
    both_own = jnp.stack([as_band(trajectory[0]), obs_own])
    prec_own = as_band(error_precision[0])

    y_own = as_band(error_precision[0] * departures[0])
    y_all = [y_own, swap(y_own, 1), swap(y_own, 2), swap(y_own, 3)]
    b_all = by_partner(both_own)
    p_all = by_partner(prec_own)
    y_later = along_tm(jnp.stack(y_all), -1)
    p_later = along_tm(jnp.stack(p_all), -1)

    fore_in, fore_out = stack_in(conv_in), stack_out(conv_out)
    back_in, back_out = stack_in(flipped(conv_out)), stack_out(flipped(conv_in))
    taps = pltpu.VMEM((ROWS, TAPS, lon), BF16)
    hidden = pltpu.VMEM((ROWS + 2, hid, lon), BF16)
    field = pltpu.VMEM((BANDS, PAIR, lon), F32)

    gate_shape = shape_b(ROWS, hid, lon)
    gate, r0, r0_b = call(
        rhs_kernel,
        "rhs",
        (step_counts, *y_all, y_later, *b_all, fore_in, hidden_bias[:, None], back_in, back_out),
        [gate_shape, whole, whole_b],
        [field, taps, hidden],
        1,
    )
    later = along_tm(r0_b, -1)
    z1, z1_b = call(
        forward_kernel,
        "forward",
        (step_counts, r0, gate, fore_in, fore_out),
        [whole, whole_b],
        [taps, hidden],
        1,
    )
    earlier = along_tm(z1_b, 1)
    observed, pick, spread, weights = call(
        observe_kernel,
        "observe",
        (z1, *b_all),
        [
            whole,
            shape_b(BANDS, 2 * TILE, SLOTS),
            shape_b(BANDS, SLOTS, 2 * TILE),
            shape(BANDS, 2 * TILE, TILE),
        ],
    )
    (adjoint,) = call(
        adjoint_kernel,
        "adjoint",
        (step_counts, observed, z1, later, p_later, gate, back_in, back_out),
        [whole],
        [taps, hidden],
        1,
    )
    v1, v1_b = call(image_kernel, "image", (r0, earlier, adjoint, *p_all), [whole, whole_b])
    later = along_tm(v1_b, -1)
    z2, z2_b = call(
        forward_kernel,
        "forward",
        (step_counts, v1, gate, fore_in, fore_out),
        [whole, whole_b],
        [taps, hidden],
        1,
    )
    earlier = along_tm(z2_b, 1)
    observed, energy = call(
        observe_again_kernel,
        "observe_again",
        (z2, pick, spread, weights),
        [whole, shape(8, TILE)],
    )
    (dots,) = call(
        products_kernel,
        "products",
        (r0, v1, z2, later, p_later, *p_all, energy),
        [shape(8, TILE)],
    )
    count = lax.axis_size("tm")
    parts = [dots] + [
        lax.ppermute(dots, "tm", [(i, i ^ step) for i in range(count)]) for step in range(1, count)
    ]
    observed, _ = lax.optimization_barrier((observed, dots))
    (adjoint,) = call(
        adjoint_kernel,
        "adjoint",
        (step_counts, observed, z2, later, p_later, gate, back_in, back_out),
        [whole],
        [taps, hidden],
        1,
    )
    inc, res = call(
        finish_kernel,
        "finish",
        (*parts, r0, v1, earlier, adjoint, p_all[0]),
        [shape(chan, rows, lon)] * 2,
    )
    return (jnp.transpose(inc, (1, 0, 2))[None], jnp.transpose(res, (1, 0, 2))[None])


def solution(mesh):
    in_specs = (
        P(("ens", "tm"), "lat", None, None),
        P(("ens", "tm"), "lat", None, None),
        P(("ens", "tm"), "lat", None, None),
        P(),
        P(),
        P(),
        P(("ens", "tm")),
        P(("ens", "tm"), "lat"),
        P(("ens", "tm"), "lat", None),
        P(("ens", "tm"), "lat"),
        P(("ens", "tm"), "lat"),
    )
    out_specs = (P(("ens", "tm"), "lat", None, None), P(("ens", "tm"), "lat", None, None))
    plan = row_plan if mesh.shape["lat"] == BANDS and mesh.shape["tm"] == 4 else halo_plan
    return jax.shard_map(plan, mesh=mesh, in_specs=in_specs, out_specs=out_specs, check_vma=False)
```

```python
import functools

import jax
import jax.numpy as jnp
from jax import lax
from jax.experimental import pallas as pl
from jax.experimental.pallas import tpu as pltpu
from jax.sharding import PartitionSpec as P

TILE = 128
STEPS = 2
ITERS = 2
F32 = jnp.float32
BF16 = jnp.bfloat16


def padded_2(cells, sides, width):
    for axis, dim in sides:
        count = lax.axis_size(axis)
        ends = count - 1
        head = lax.slice_in_dim(cells, 0, width, axis=dim)
        tail = lax.slice_in_dim(cells, cells.shape[dim] - width, cells.shape[dim], axis=dim)
        cells = jnp.concatenate(
            [
                lax.ppermute(tail, axis, [(i, (i + 1) % count) for i in range(ends)]),
                cells,
                lax.ppermute(head, axis, [((i + 1) % count, i) for i in range(ends)]),
            ],
            axis=dim,
        )
    return cells


def from_behind(value, axis, steps):
    count = lax.axis_size(axis)
    leading, last = (max(0, -steps), min(count, count - steps))
    return lax.ppermute(value, axis, [(source, source + steps) for source in range(leading, last)])


def convolve_padded(padded, kernel):
    out_rows = padded.shape[0] - 2
    lon_len = padded.shape[2]
    wrapped = jnp.concatenate([padded[:, :, -1:], padded, padded[:, :, :1]], axis=2)
    accumulated = None
    for row_off in range(3):
        for col_off in range(3):
            window = wrapped[row_off : row_off + out_rows, :, col_off : col_off + lon_len]
            term = jnp.einsum(
                "oi,ril->rol", kernel[row_off, col_off], window, preferred_element_type=F32
            )
            accumulated = term if accumulated is None else accumulated + term
    return accumulated


def flipped(kernel):
    return jnp.transpose(kernel[::-1, ::-1], (0, 1, 3, 2))


def rim_wide(source):
    return padded_2(source, (("lat", 0),), 2)


def shift_up(source):
    return from_behind(source.astype(BF16), "tm", -1).astype(source.dtype)


def global_squares(source):
    return lax.psum(jnp.sum(source * source), ("tm", "lat"))


def halo_plan(
    departures,
    error_precision,
    trajectory,
    conv_in,
    conv_out,
    hidden_bias,
    step_counts,
    obs_tiles,
    obs_weights,
    innovations,
    obs_precision,
):
    precision = error_precision[0]
    own_count = step_counts[0]
    tile_index = obs_tiles[0]
    weights = obs_weights[0]
    innovation = innovations[0]
    obs_scale = obs_precision[0]
    back_in = flipped(conv_in)
    back_out = flipped(conv_out)
    trajectory_ext = padded_2(trajectory[0], (("lat", 0),), 1)
    gate_factor = (
        1.0 - jnp.tanh(convolve_padded(trajectory_ext, conv_in) + hidden_bias[:, None]) ** 2
    ).astype(BF16)
    gate_wide = padded_2(gate_factor, (("lat", 0),), 1)

    def one_step(current, first_kernel, second_kernel):
        widened = rim_wide(current.astype(BF16))
        hidden = (gate_wide.astype(F32) * convolve_padded(widened, first_kernel)).astype(BF16)
        return current + convolve_padded(hidden, second_kernel)

    def model(current, first_kernel, second_kernel):
        for step_index in range(STEPS):
            current = jnp.where(
                step_index < own_count, one_step(current, first_kernel, second_kernel), current
            )
        return current

    def observe_adjoint(scaled, like):
        tile_table = (
            jnp.zeros((like.size // TILE, TILE), F32)
            .at[tile_index]
            .add(weights * scaled[:, None])
        )
        return tile_table.reshape(like.shape)

    first_weighted = precision * departures[0]
    rhs = first_weighted + model(
        observe_adjoint(obs_scale * innovation, first_weighted) - shift_up(first_weighted),
        back_out,
        back_in,
    )
    increment = jnp.zeros_like(rhs)
    residual = rhs
    direction = rhs
    norm_now = global_squares(residual)
    for _ in range(ITERS):
        propagated = model(direction, conv_in, conv_out)
        earlier = from_behind(propagated.astype(BF16), "tm", 1).astype(F32)
        weighted = precision * (direction - earlier)
        picked = propagated.reshape(-1, TILE)[tile_index]
        observed = jnp.sum(picked * weights, axis=1)
        operator_image = weighted + model(
            observe_adjoint(obs_scale * observed, direction) - shift_up(weighted),
            back_out,
            back_in,
        )
        curvature = lax.psum(jnp.sum(direction * operator_image), ("tm", "lat"))
        step_length = norm_now / curvature
        increment = increment + step_length * direction
        residual = residual - step_length * operator_image
        norm_next = global_squares(residual)
        direction = residual + norm_next / norm_now * direction
        norm_now = norm_next
    return (increment[None], residual[None])


BANDS = 4
ROWS = 2 * BANDS
CHAN = 72
CHAN_IN = 80
TAPS = 256
PAIR = 2 * CHAN
SLOTS = 4 * CHAN
OBS_ROWS = 144
SHRINK = 2.0**-16


def row_of(ref, row):
    return ref[row // 2, (row % 2) * CHAN : (row % 2 + 1) * CHAN, :]


def taps_of(row):
    zeros = jnp.zeros((CHAN_IN - CHAN, row.shape[1]), F32)
    right = pltpu.roll(row, 1, axis=1)
    left = pltpu.roll(row, row.shape[1] - 1, axis=1)
    return jnp.concatenate([right, zeros, row, zeros, left, zeros], axis=0).astype(BF16)


def clear_taps(taps):
    used = 3 * CHAN_IN
    taps[:, used:, :] = jnp.zeros((ROWS, TAPS - used, taps.shape[2]), BF16)


def conv_rows(field, w_in, taps, emit):
    for row in range(ROWS):
        taps[row, : 3 * CHAN_IN] = taps_of(row_of(field, row))
    for row in range(ROWS):
        low, high = max(row - 1, 0), min(row + 2, ROWS)
        stacked = taps[low:high].reshape((high - low) * TAPS, taps.shape[2])
        skip = (low - (row - 1)) * TAPS
        weights = w_in[:, skip : skip + (high - low) * TAPS]
        emit(row, jnp.dot(weights, stacked, preferred_element_type=F32))


def prepare(taps, hidden):
    clear_taps(taps)
    hidden[0] = jnp.zeros(hidden.shape[1:], BF16)
    hidden[ROWS + 1] = jnp.zeros(hidden.shape[1:], BF16)


def model_step(source, target, target_b, gate, w_in, w_out, taps, hidden):
    def gated(row, value):
        hidden[row + 1] = (gate[row].astype(F32) * value).astype(BF16)

    conv_rows(source, w_in, taps, gated)
    for pair in range(BANDS):
        stacked = hidden[2 * pair : 2 * pair + 4].reshape(-1, hidden.shape[2])
        part = jnp.dot(w_out[...], stacked, preferred_element_type=F32)
        lon = part.shape[1]
        rows = []
        for row in range(2):
            tap = [part[(3 * row + b) * CHAN : (3 * row + b + 1) * CHAN] for b in range(3)]
            spread = pltpu.roll(tap[0], 1, axis=1) + tap[1] + pltpu.roll(tap[2], lon - 1, axis=1)
            rows.append(source[pair, row * CHAN : (row + 1) * CHAN, :] + spread)
        band = jnp.concatenate(rows, axis=0)
        target[pair] = band
        if target_b is not None:
            target_b[pair] = band.astype(BF16)


def model_steps(field, gate, w_in, w_out, taps, hidden, count):
    prepare(taps, hidden)

    def one_step(_, carry):
        model_step(field, field, None, gate, w_in, w_out, taps, hidden)
        return carry

    lax.fori_loop(0, jnp.minimum(count, STEPS), one_step, 0)


def forward_steps(start, out, out_b, gate, w_in, w_out, taps, hidden, count):
    prepare(taps, hidden)
    model_step(start, out, out_b, gate, w_in, w_out, taps, hidden)

    def one_step(_, carry):
        model_step(out, out, out_b, gate, w_in, w_out, taps, hidden)
        return carry

    lax.fori_loop(1, jnp.minimum(count, STEPS), one_step, 0)


def split_16(value):
    high = value.astype(BF16)
    low = (value - high.astype(F32)).astype(BF16)
    return high, low


def obs_of(obs):
    weights = jnp.concatenate([obs[:TILE, :TILE], obs[:TILE, TILE:]], axis=0)
    extra = obs[TILE:, :].astype(F32)
    return weights, 2.0 * extra[0:1] + extra[1:2], extra[2:3], extra[3:4]


def one_hot_t(slot):
    iota = lax.broadcasted_iota(jnp.int32, (SLOTS, 2 * TILE), 0).astype(F32)
    return (iota == slot).astype(F32)


def one_hot(slot):
    columns = [
        jnp.transpose(jnp.broadcast_to(slot[:, half * TILE : (half + 1) * TILE], (TILE, TILE)))[:, :1]
        for half in range(2)
    ]
    column = jnp.concatenate(columns, axis=0)
    iota = lax.broadcasted_iota(jnp.int32, (2 * TILE, SLOTS), 1).astype(F32)
    return (iota == column).astype(F32)


def band_slots(band):
    return jnp.concatenate(
        [
            band[row * CHAN : (row + 1) * CHAN, half * TILE : (half + 1) * TILE]
            for row in range(2)
            for half in range(2)
        ],
        axis=0,
    )


def slots_band(slots):
    return jnp.concatenate(
        [
            jnp.concatenate(
                [slots[(2 * row + half) * CHAN : (2 * row + half + 1) * CHAN] for half in range(2)],
                axis=1,
            )
            for row in range(2)
        ],
        axis=0,
    )


def rhs_kernel(
    counts,
    y0, y1, y2, y3,
    later,
    b0, b1, b2, b3,
    fore_in, bias, w_in, w_out,
    gate, out, out_b,
    field, taps, hidden,
):
    me = lax.axis_index("lat")
    more = lax.axis_index("tm") < lax.axis_size("tm") - 1
    blocks = (b0, b1, b2, b3)
    for shift, block in enumerate(blocks):
        field[me ^ shift] = block[0].astype(F32)
    prepare(taps, hidden)

    def emit(row, value):
        squashed = jnp.tanh(value + bias[...])
        gate[row] = (1.0 - squashed * squashed).astype(BF16)

    conv_rows(field, fore_in, taps, emit)
    for shift, block in enumerate(blocks):
        weights, slot, high, low = obs_of(block[1])
        hot = one_hot_t(slot)
        both = jnp.concatenate([hot * high, hot * low], axis=1).astype(BF16)
        slots = jnp.dot(
            both, jnp.concatenate([weights, weights], axis=0), preferred_element_type=F32
        )
        next_y = jnp.where(more, later[shift].astype(F32), 0.0)
        field[me ^ shift] = slots_band(slots) - next_y

    def one_step(_, carry):
        model_step(field, field, None, gate, w_in, w_out, taps, hidden)
        return carry

    lax.fori_loop(0, jnp.minimum(counts[0], STEPS), one_step, 0)
    for shift, block in enumerate((y0, y1, y2, y3)):
        total = field[me ^ shift] + block[...].astype(F32)
        out[me ^ shift] = total
        out_b[me ^ shift] = total.astype(BF16)


def forward_kernel(counts, start, gate, w_in, w_out, out, out_b, taps, hidden):
    forward_steps(start, out, out_b, gate, w_in, w_out, taps, hidden, counts[0])


def observed_band(z_band, pick, spread, weights):
    ones = jnp.ones((2 * TILE, TILE), BF16)

    def product(left, value):
        return jnp.dot(left, jnp.concatenate(split_16(value), axis=1), preferred_element_type=F32)

    picked = product(pick, band_slots(z_band))
    terms = (picked[:, :TILE] + picked[:, TILE:]) * weights
    terms = jnp.concatenate(split_16(terms), axis=1)
    scaled = jnp.dot(terms, ones, preferred_element_type=F32)
    slots = product(spread, weights * scaled)
    squares = jnp.sum(scaled * scaled, axis=0, keepdims=True)
    return slots_band(slots[:, :TILE] + slots[:, TILE:]), squares


def observe_kernel(z, b0, b1, b2, b3, out, pick, spread, weights):
    me = lax.axis_index("lat")
    for shift, block in enumerate((b0, b1, b2, b3)):
        at = me ^ shift
        own, slot, _, _ = obs_of(block[1])
        pick[at] = one_hot(slot).astype(BF16)
        spread[at] = one_hot_t(slot).astype(BF16)
        weights[at] = own.astype(F32)
    for band in range(BANDS):
        out[band], _ = observed_band(z[band], pick[band], spread[band], weights[band])


def observe_again_kernel(z, pick, spread, weights, out, energy):
    squares = jnp.zeros((1, TILE), F32)
    for band in range(BANDS):
        out[band], own = observed_band(z[band], pick[band], spread[band], weights[band])
        squares = squares + own
    energy[...] = jnp.broadcast_to(squares, energy.shape)


def next_misfit(at, shift, later, z, precision):
    more = lax.axis_index("tm") < lax.axis_size("tm") - 1
    weight = jnp.where(more, precision[shift].astype(F32), 0.0)
    return later[at].astype(F32) - z[at], weight


def adjoint_kernel(
    counts, observed, z, later, precision, gate, w_in, w_out, field, taps, hidden
):
    me = lax.axis_index("lat")
    for shift in range(BANDS):
        at = me ^ shift
        misfit, weight = next_misfit(at, shift, later, z, precision)
        field[at] = observed[at] - weight * misfit
    model_steps(field, gate, w_in, w_out, taps, hidden, counts[0])


def image_of(at, block, start, earlier, adjoint):
    before = jnp.where(lax.axis_index("tm") == 0, 0.0, earlier[at].astype(F32))
    return block.astype(F32) * (start[at] - before) + adjoint[at]


def image_kernel(start, earlier, adjoint, p0, p1, p2, p3, out, out_b):
    me = lax.axis_index("lat")
    for shift, block in enumerate((p0, p1, p2, p3)):
        at = me ^ shift
        total = SHRINK * image_of(at, block[...], start, earlier, adjoint)
        out[at] = total
        out_b[at] = total.astype(BF16)


def products_kernel(first, second, z, later, precision, p0, p1, p2, p3, energy, dots):
    me = lax.axis_index("lat")
    tm_first = lax.axis_index("tm") == 0
    most = jnp.max(jnp.max(jnp.abs(second[...]), axis=0), axis=0, keepdims=True)
    most = jnp.maximum(jnp.max(most, axis=1, keepdims=True), 1e-30)
    inverse = jnp.broadcast_to(1.0 / most, (1, first.shape[2]))
    sums = [jnp.zeros((1, first.shape[2]), F32) for _ in range(4)]
    for shift, block in enumerate((p0, p1, p2, p3)):
        at = me ^ shift
        r0, v1 = first[at], second[at]
        misfit, weight = next_misfit(at, shift, later, z, precision)
        initial = jnp.where(tm_first, block[...].astype(F32), 0.0)
        near, far = v1 * inverse, misfit * inverse
        square = near * near
        terms = (r0 * r0, r0 * v1, square, weight * far * far + initial * square)
        sums = [total + jnp.sum(term, axis=0, keepdims=True) for total, term in zip(sums, terms)]
    for j, total in enumerate(sums):
        value = jnp.broadcast_to(jnp.sum(total, axis=1, keepdims=True), (1, TILE))
        dots[j : j + 1, :] = value + energy[:1, :] * (inverse * inverse)[:, :TILE] if j == 3 else value
    dots[4:5, :] = jnp.broadcast_to(most, (1, TILE))
    dots[5:8, :] = jnp.zeros((3, TILE), F32)


def finish_kernel(d0, d1, d2, d3, first, second, earlier, adjoint, p0, inc, res):
    me = lax.axis_index("lat")
    chan, _, lon = inc.shape
    shares = [d[...] for d in (d0, d1, d2, d3)]
    mosts = [share[4:5, :1] for share in shares]
    most = jnp.maximum(jnp.maximum(mosts[0], mosts[1]), jnp.maximum(mosts[2], mosts[3]))
    added = lambda values: (values[0] + values[1]) + (values[2] + values[3])
    rr0 = added([share[0:1, :1] for share in shares])
    c0 = added([share[1:2, :1] for share in shares]) / SHRINK
    g11, g12 = [
        added([share[j : j + 1, :1] * (own / most) * (own / most) for share, own in zip(shares, mosts)])
        for j in (2, 3)
    ]
    a0 = rr0 / c0
    full = most / SHRINK
    reach = a0 * full
    rr1 = rr0 - 2.0 * a0 * c0 + reach * reach * g11
    beta = rr1 / rr0
    grow = 1.0 + beta
    c1 = grow * grow * c0 - 2.0 * grow * reach * full * g11 + reach * reach * g12
    a1 = rr1 / c1
    wide = lambda value: jnp.broadcast_to(value, (chan, lon))
    step, cross = wide(a0 + a1 * grow), wide(a1 * a0 / SHRINK)
    along = step / SHRINK
    image = image_of(me, p0[...], second, earlier, adjoint)
    r0_own, v1_own = first[me], second[me]
    for row in range(2):
        at = row * CHAN
        r0, v1, v2 = [field[at : at + chan] for field in (r0_own, v1_own, image)]
        inc[:, row, :] = step * r0 - cross * v1
        res[:, row, :] = r0 - along * v1 + cross * v2


VMEM = pl.BlockSpec(memory_space=pltpu.VMEM)
SMEM = pl.BlockSpec(memory_space=pltpu.SMEM)


def call(kernel, name, ins, outs, scratch=(), scalars=0):
    specs = [SMEM] * scalars + [VMEM] * (len(ins) - scalars)
    return pl.pallas_call(
        kernel,
        name=name,
        out_shape=outs,
        in_specs=specs,
        out_specs=[VMEM] * len(outs),
        scratch_shapes=list(scratch),
        compiler_params=pltpu.CompilerParams(vmem_limit_bytes=48 << 20),
        cost_estimate=pl.CostEstimate(flops=1, bytes_accessed=1, transcendentals=0),
    )(*ins)


def stack_in(kernel):
    rows, cols, out_c, in_c = kernel.shape
    padded = jnp.pad(kernel, ((0, 0), (0, 0), (0, 0), (0, CHAN_IN - in_c)))
    block = jnp.transpose(padded, (2, 0, 1, 3)).reshape(out_c, rows, cols * CHAN_IN)
    block = jnp.pad(block, ((0, 0), (0, 0), (0, TAPS - cols * CHAN_IN)))
    return block.reshape(out_c, rows * TAPS)


def stack_out(kernel):
    rows, cols, out_c, in_c = kernel.shape
    padded = jnp.pad(kernel, ((0, 0), (0, 0), (0, CHAN - out_c), (0, 0)))
    none = jnp.zeros_like(padded[0])
    tap = lambda row_off: padded[row_off] if 0 <= row_off < rows else none
    blocks = [jnp.concatenate([tap(t - m) for t in range(4)], axis=-1) for m in range(2)]
    return jnp.concatenate(blocks, axis=0).reshape(2 * cols * CHAN, 4 * in_c)


def as_band(cells):
    rows, chan, lon = cells.shape
    return jnp.pad(cells.astype(BF16), ((0, 0), (0, CHAN - chan), (0, 0))).reshape(PAIR, lon)


def swap(block, shift):
    count = lax.axis_size("lat")
    return lax.ppermute(block, "lat", [(i, i ^ shift) for i in range(count)])


def by_partner(value):
    far = swap(value, 2)
    return [value, swap(value, 1), far, swap(far, 1)]


def along_tm(value, step):
    count = lax.axis_size("tm")
    return lax.ppermute(value, "tm", [(i, (i + step) % count) for i in range(count)])


def row_plan(
    departures,
    error_precision,
    trajectory,
    conv_in,
    conv_out,
    hidden_bias,
    step_counts,
    obs_tiles,
    obs_weights,
    innovations,
    obs_precision,
):
    _, rows, chan, lon = departures.shape
    hid = conv_in.shape[2]
    shape = lambda *dims: jax.ShapeDtypeStruct(dims, F32)
    shape_b = lambda *dims: jax.ShapeDtypeStruct(dims, BF16)
    whole, whole_b = shape(BANDS, PAIR, lon), shape_b(BANDS, PAIR, lon)

    root = jnp.sqrt(obs_precision[0])
    tiles = obs_tiles[0]
    per_row = 2 * chan
    slot = (2 * (tiles // per_row) + tiles % 2) * CHAN + (tiles // 2) % chan
    innov_high, innov_low = split_16(root * innovations[0])
    table = lambda value: value.astype(BF16).reshape(1, 2 * TILE)
    weights = (obs_weights[0] * root[:, None]).astype(BF16)
    obs_own = jnp.concatenate(
        [
            jnp.concatenate([weights[:TILE], weights[TILE:]], axis=1),
            table(slot // 2),
            table(slot % 2),
            table(innov_high),
            table(innov_low),
            jnp.zeros((OBS_ROWS - TILE - 4, 2 * TILE), BF16),
        ],
        axis=0,
    )
    both_own = jnp.stack([as_band(trajectory[0]), obs_own])
    prec_own = as_band(error_precision[0])

    y_own = as_band(error_precision[0] * departures[0])
    y_all = [y_own, swap(y_own, 1), swap(y_own, 2), swap(y_own, 3)]
    b_all = by_partner(both_own)
    p_all = by_partner(prec_own)
    y_later = along_tm(jnp.stack(y_all), -1)
    p_later = along_tm(jnp.stack(p_all), -1)

    fore_in, fore_out = stack_in(conv_in), stack_out(conv_out)
    back_in, back_out = stack_in(flipped(conv_out)), stack_out(flipped(conv_in))
    taps = pltpu.VMEM((ROWS, TAPS, lon), BF16)
    hidden = pltpu.VMEM((ROWS + 2, hid, lon), BF16)
    field = pltpu.VMEM((BANDS, PAIR, lon), F32)

    gate_shape = shape_b(ROWS, hid, lon)
    gate, r0, r0_b = call(
        rhs_kernel,
        "rhs",
        (step_counts, *y_all, y_later, *b_all, fore_in, hidden_bias[:, None], back_in, back_out),
        [gate_shape, whole, whole_b],
        [field, taps, hidden],
        1,
    )
    later = along_tm(r0_b, -1)
    z1, z1_b = call(
        forward_kernel,
        "forward",
        (step_counts, r0, gate, fore_in, fore_out),
        [whole, whole_b],
        [taps, hidden],
        1,
    )
    earlier = along_tm(z1_b, 1)
    observed, pick, spread, weights = call(
        observe_kernel,
        "observe",
        (z1, *b_all),
        [
            whole,
            shape_b(BANDS, 2 * TILE, SLOTS),
            shape_b(BANDS, SLOTS, 2 * TILE),
            shape(BANDS, 2 * TILE, TILE),
        ],
    )
    (adjoint,) = call(
        adjoint_kernel,
        "adjoint",
        (step_counts, observed, z1, later, p_later, gate, back_in, back_out),
        [whole],
        [taps, hidden],
        1,
    )
    v1, v1_b = call(image_kernel, "image", (r0, earlier, adjoint, *p_all), [whole, whole_b])
    later = along_tm(v1_b, -1)
    z2, z2_b = call(
        forward_kernel,
        "forward",
        (step_counts, v1, gate, fore_in, fore_out),
        [whole, whole_b],
        [taps, hidden],
        1,
    )
    earlier = along_tm(z2_b, 1)
    observed, energy = call(
        observe_again_kernel,
        "observe_again",
        (z2, pick, spread, weights),
        [whole, shape(8, TILE)],
    )
    (dots,) = call(
        products_kernel,
        "products",
        (r0, v1, z2, later, p_later, *p_all, energy),
        [shape(8, TILE)],
    )
    count = lax.axis_size("tm")
    parts = [dots] + [
        lax.ppermute(dots, "tm", [(i, i ^ step) for i in range(count)]) for step in range(1, count)
    ]
    observed, _ = lax.optimization_barrier((observed, dots))
    (adjoint,) = call(
        adjoint_kernel,
        "adjoint",
        (step_counts, observed, z2, later, p_later, gate, back_in, back_out),
        [whole],
        [taps, hidden],
        1,
    )
    inc, res = call(
        finish_kernel,
        "finish",
        (*parts, r0, v1, earlier, adjoint, p_all[0]),
        [shape(chan, rows, lon)] * 2,
    )
    return (jnp.transpose(inc, (1, 0, 2))[None], jnp.transpose(res, (1, 0, 2))[None])


def solution(mesh):
    in_specs = (
        P(("ens", "tm"), "lat", None, None),
        P(("ens", "tm"), "lat", None, None),
        P(("ens", "tm"), "lat", None, None),
        P(),
        P(),
        P(),
        P(("ens", "tm")),
        P(("ens", "tm"), "lat"),
        P(("ens", "tm"), "lat", None),
        P(("ens", "tm"), "lat"),
        P(("ens", "tm"), "lat"),
    )
    out_specs = (P(("ens", "tm"), "lat", None, None), P(("ens", "tm"), "lat", None, None))
    plan = row_plan if mesh.shape["lat"] == BANDS and mesh.shape["tm"] == 4 else halo_plan
    return jax.shard_map(plan, mesh=mesh, in_specs=in_specs, out_specs=out_specs, check_vma=False)
```

```python
import functools

import jax
import jax.numpy as jnp
from jax import lax
from jax.experimental import pallas as pl
from jax.experimental.pallas import tpu as pltpu
from jax.sharding import PartitionSpec as P

TILE = 128
STEPS = 2
ITERS = 2
F32 = jnp.float32
BF16 = jnp.bfloat16


def padded_2(cells, sides, width):
    for axis, dim in sides:
        count = lax.axis_size(axis)
        ends = count - 1
        head = lax.slice_in_dim(cells, 0, width, axis=dim)
        tail = lax.slice_in_dim(cells, cells.shape[dim] - width, cells.shape[dim], axis=dim)
        cells = jnp.concatenate(
            [
                lax.ppermute(tail, axis, [(i, (i + 1) % count) for i in range(ends)]),
                cells,
                lax.ppermute(head, axis, [((i + 1) % count, i) for i in range(ends)]),
            ],
            axis=dim,
        )
    return cells


def from_behind(value, axis, steps):
    count = lax.axis_size(axis)
    leading, last = (max(0, -steps), min(count, count - steps))
    return lax.ppermute(value, axis, [(source, source + steps) for source in range(leading, last)])


def convolve_padded(padded, kernel):
    out_rows = padded.shape[0] - 2
    lon_len = padded.shape[2]
    wrapped = jnp.concatenate([padded[:, :, -1:], padded, padded[:, :, :1]], axis=2)
    accumulated = None
    for row_off in range(3):
        for col_off in range(3):
            window = wrapped[row_off : row_off + out_rows, :, col_off : col_off + lon_len]
            term = jnp.einsum(
                "oi,ril->rol", kernel[row_off, col_off], window, preferred_element_type=F32
            )
            accumulated = term if accumulated is None else accumulated + term
    return accumulated


def flipped(kernel):
    return jnp.transpose(kernel[::-1, ::-1], (0, 1, 3, 2))


def rim_wide(source):
    return padded_2(source, (("lat", 0),), 2)


def shift_up(source):
    return from_behind(source.astype(BF16), "tm", -1).astype(source.dtype)


def global_squares(source):
    return lax.psum(jnp.sum(source * source), ("tm", "lat"))


def halo_plan(
    departures,
    error_precision,
    trajectory,
    conv_in,
    conv_out,
    hidden_bias,
    step_counts,
    obs_tiles,
    obs_weights,
    innovations,
    obs_precision,
):
    precision = error_precision[0]
    own_count = step_counts[0]
    tile_index = obs_tiles[0]
    weights = obs_weights[0]
    innovation = innovations[0]
    obs_scale = obs_precision[0]
    back_in = flipped(conv_in)
    back_out = flipped(conv_out)
    trajectory_ext = padded_2(trajectory[0], (("lat", 0),), 1)
    gate_factor = (
        1.0 - jnp.tanh(convolve_padded(trajectory_ext, conv_in) + hidden_bias[:, None]) ** 2
    ).astype(BF16)
    gate_wide = padded_2(gate_factor, (("lat", 0),), 1)

    def one_step(current, first_kernel, second_kernel):
        widened = rim_wide(current.astype(BF16))
        hidden = (gate_wide.astype(F32) * convolve_padded(widened, first_kernel)).astype(BF16)
        return current + convolve_padded(hidden, second_kernel)

    def model(current, first_kernel, second_kernel):
        for step_index in range(STEPS):
            current = jnp.where(
                step_index < own_count, one_step(current, first_kernel, second_kernel), current
            )
        return current

    def observe_adjoint(scaled, like):
        tile_table = (
            jnp.zeros((like.size // TILE, TILE), F32)
            .at[tile_index]
            .add(weights * scaled[:, None])
        )
        return tile_table.reshape(like.shape)

    first_weighted = precision * departures[0]
    rhs = first_weighted + model(
        observe_adjoint(obs_scale * innovation, first_weighted) - shift_up(first_weighted),
        back_out,
        back_in,
    )
    increment = jnp.zeros_like(rhs)
    residual = rhs
    direction = rhs
    norm_now = global_squares(residual)
    for _ in range(ITERS):
        propagated = model(direction, conv_in, conv_out)
        earlier = from_behind(propagated.astype(BF16), "tm", 1).astype(F32)
        weighted = precision * (direction - earlier)
        picked = propagated.reshape(-1, TILE)[tile_index]
        observed = jnp.sum(picked * weights, axis=1)
        operator_image = weighted + model(
            observe_adjoint(obs_scale * observed, direction) - shift_up(weighted),
            back_out,
            back_in,
        )
        curvature = lax.psum(jnp.sum(direction * operator_image), ("tm", "lat"))
        step_length = norm_now / curvature
        increment = increment + step_length * direction
        residual = residual - step_length * operator_image
        norm_next = global_squares(residual)
        direction = residual + norm_next / norm_now * direction
        norm_now = norm_next
    return (increment[None], residual[None])


BANDS = 4
ROWS = 2 * BANDS
CHAN = 72
CHAN_IN = 80
TAPS = 256
PAIR = 2 * CHAN
SLOTS = 4 * CHAN
OBS_ROWS = 144
SHRINK = 2.0**-16


def row_of(ref, row):
    return ref[row // 2, (row % 2) * CHAN : (row % 2 + 1) * CHAN, :]


def taps_of(row):
    zeros = jnp.zeros((CHAN_IN - CHAN, row.shape[1]), F32)
    right = pltpu.roll(row, 1, axis=1)
    left = pltpu.roll(row, row.shape[1] - 1, axis=1)
    return jnp.concatenate([right, zeros, row, zeros, left, zeros], axis=0).astype(BF16)


def clear_taps(taps):
    used = 3 * CHAN_IN
    taps[:, used:, :] = jnp.zeros((ROWS, TAPS - used, taps.shape[2]), BF16)


def conv_rows(field, w_in, taps, emit):
    for row in range(ROWS):
        taps[row, : 3 * CHAN_IN] = taps_of(row_of(field, row))
    for row in range(ROWS):
        low, high = max(row - 1, 0), min(row + 2, ROWS)
        stacked = taps[low:high].reshape((high - low) * TAPS, taps.shape[2])
        skip = (low - (row - 1)) * TAPS
        weights = w_in[:, skip : skip + (high - low) * TAPS]
        emit(row, jnp.dot(weights, stacked, preferred_element_type=F32))


def prepare(taps, hidden):
    clear_taps(taps)
    hidden[0] = jnp.zeros(hidden.shape[1:], BF16)
    hidden[ROWS + 1] = jnp.zeros(hidden.shape[1:], BF16)


def model_step(source, target, target_b, gate, w_in, w_out, taps, hidden):
    def gated(row, value):
        hidden[row + 1] = (gate[row].astype(F32) * value).astype(BF16)

    conv_rows(source, w_in, taps, gated)
    for pair in range(BANDS):
        stacked = hidden[2 * pair : 2 * pair + 4].reshape(-1, hidden.shape[2])
        part = jnp.dot(w_out[...], stacked, preferred_element_type=F32)
        lon = part.shape[1]
        rows = []
        for row in range(2):
            tap = [part[(3 * row + b) * CHAN : (3 * row + b + 1) * CHAN] for b in range(3)]
            spread = pltpu.roll(tap[0], 1, axis=1) + tap[1] + pltpu.roll(tap[2], lon - 1, axis=1)
            rows.append(source[pair, row * CHAN : (row + 1) * CHAN, :] + spread)
        band = jnp.concatenate(rows, axis=0)
        target[pair] = band
        if target_b is not None:
            target_b[pair] = band.astype(BF16)


def model_steps(field, gate, w_in, w_out, taps, hidden, count):
    prepare(taps, hidden)

    def one_step(_, carry):
        model_step(field, field, None, gate, w_in, w_out, taps, hidden)
        return carry

    lax.fori_loop(0, jnp.minimum(count, STEPS), one_step, 0)


def forward_steps(start, out, out_b, gate, w_in, w_out, taps, hidden, count):
    prepare(taps, hidden)
    model_step(start, out, out_b, gate, w_in, w_out, taps, hidden)

    def one_step(_, carry):
        model_step(out, out, out_b, gate, w_in, w_out, taps, hidden)
        return carry

    lax.fori_loop(1, jnp.minimum(count, STEPS), one_step, 0)


def split_16(value):
    high = value.astype(BF16)
    low = (value - high.astype(F32)).astype(BF16)
    return high, low


def obs_of(obs):
    weights = jnp.concatenate([obs[:TILE, :TILE], obs[:TILE, TILE:]], axis=0)
    extra = obs[TILE:, :].astype(F32)
    return weights, 2.0 * extra[0:1] + extra[1:2], extra[2:3], extra[3:4]


def one_hot_t(slot):
    iota = lax.broadcasted_iota(jnp.int32, (SLOTS, 2 * TILE), 0).astype(F32)
    return (iota == slot).astype(F32)


def one_hot(slot):
    columns = [
        jnp.transpose(jnp.broadcast_to(slot[:, half * TILE : (half + 1) * TILE], (TILE, TILE)))[:, :1]
        for half in range(2)
    ]
    column = jnp.concatenate(columns, axis=0)
    iota = lax.broadcasted_iota(jnp.int32, (2 * TILE, SLOTS), 1).astype(F32)
    return (iota == column).astype(F32)


def band_slots(band):
    return jnp.concatenate(
        [
            band[row * CHAN : (row + 1) * CHAN, half * TILE : (half + 1) * TILE]
            for row in range(2)
            for half in range(2)
        ],
        axis=0,
    )


def slots_band(slots):
    return jnp.concatenate(
        [
            jnp.concatenate(
                [slots[(2 * row + half) * CHAN : (2 * row + half + 1) * CHAN] for half in range(2)],
                axis=1,
            )
            for row in range(2)
        ],
        axis=0,
    )


def rhs_kernel(
    counts,
    y0, y1, y2, y3,
    later,
    b0, b1, b2, b3,
    fore_in, bias, w_in, w_out,
    gate, out, out_b,
    field, taps, hidden,
):
    me = lax.axis_index("lat")
    more = lax.axis_index("tm") < lax.axis_size("tm") - 1
    blocks = (b0, b1, b2, b3)
    for shift, block in enumerate(blocks):
        field[me ^ shift] = block[0].astype(F32)
    prepare(taps, hidden)

    def emit(row, value):
        squashed = jnp.tanh(value + bias[...])
        gate[row] = (1.0 - squashed * squashed).astype(BF16)

    conv_rows(field, fore_in, taps, emit)
    for shift, block in enumerate(blocks):
        weights, slot, high, low = obs_of(block[1])
        hot = one_hot_t(slot)
        both = jnp.concatenate([hot * high, hot * low], axis=1).astype(BF16)
        slots = jnp.dot(
            both, jnp.concatenate([weights, weights], axis=0), preferred_element_type=F32
        )
        next_y = jnp.where(more, later[shift].astype(F32), 0.0)
        field[me ^ shift] = slots_band(slots) - next_y

    def one_step(_, carry):
        model_step(field, field, None, gate, w_in, w_out, taps, hidden)
        return carry

    lax.fori_loop(0, jnp.minimum(counts[0], STEPS), one_step, 0)
    for shift, block in enumerate((y0, y1, y2, y3)):
        total = field[me ^ shift] + block[...].astype(F32)
        out[me ^ shift] = total
        out_b[me ^ shift] = total.astype(BF16)


def forward_kernel(counts, start, gate, w_in, w_out, out, out_b, taps, hidden):
    forward_steps(start, out, out_b, gate, w_in, w_out, taps, hidden, counts[0])


def observed_band(z_band, pick, spread, weights):
    ones = jnp.ones((2 * TILE, TILE), BF16)

    def product(left, value):
        return jnp.dot(left, jnp.concatenate(split_16(value), axis=1), preferred_element_type=F32)

    picked = product(pick, band_slots(z_band))
    terms = (picked[:, :TILE] + picked[:, TILE:]) * weights
    terms = jnp.concatenate(split_16(terms), axis=1)
    scaled = jnp.dot(terms, ones, preferred_element_type=F32)
    slots = product(spread, weights * scaled)
    most = jnp.maximum(jnp.max(jnp.abs(scaled), axis=0, keepdims=True), 1e-30)
    near = scaled * (1.0 / most)
    squares = jnp.sum(near * near, axis=0, keepdims=True)
    return slots_band(slots[:, :TILE] + slots[:, TILE:]), most, squares


def observe_kernel(z, b0, b1, b2, b3, out, pick, spread, weights):
    me = lax.axis_index("lat")
    for shift, block in enumerate((b0, b1, b2, b3)):
        at = me ^ shift
        own, slot, _, _ = obs_of(block[1])
        pick[at] = one_hot(slot).astype(BF16)
        spread[at] = one_hot_t(slot).astype(BF16)
        weights[at] = own.astype(F32)
    for band in range(BANDS):
        out[band], _, _ = observed_band(z[band], pick[band], spread[band], weights[band])


def observe_again_kernel(z, pick, spread, weights, out, energy):
    for band in range(BANDS):
        out[band], most, squares = observed_band(z[band], pick[band], spread[band], weights[band])
        energy[band : band + 1, :] = most
        energy[BANDS + band : BANDS + band + 1, :] = squares


def next_misfit(at, shift, later, z, precision):
    more = lax.axis_index("tm") < lax.axis_size("tm") - 1
    weight = jnp.where(more, precision[shift].astype(F32), 0.0)
    return later[at].astype(F32) - z[at], weight


def adjoint_kernel(
    counts, observed, z, later, precision, gate, w_in, w_out, field, taps, hidden
):
    me = lax.axis_index("lat")
    for shift in range(BANDS):
        at = me ^ shift
        misfit, weight = next_misfit(at, shift, later, z, precision)
        field[at] = observed[at] - weight * misfit
    model_steps(field, gate, w_in, w_out, taps, hidden, counts[0])


def image_of(at, block, start, earlier, adjoint):
    before = jnp.where(lax.axis_index("tm") == 0, 0.0, earlier[at].astype(F32))
    return block.astype(F32) * (start[at] - before) + adjoint[at]


def image_kernel(start, earlier, adjoint, p0, p1, p2, p3, out, out_b):
    me = lax.axis_index("lat")
    for shift, block in enumerate((p0, p1, p2, p3)):
        at = me ^ shift
        total = SHRINK * image_of(at, block[...], start, earlier, adjoint)
        out[at] = total
        out_b[at] = total.astype(BF16)


def products_kernel(first, second, z, later, precision, p0, p1, p2, p3, energy, dots):
    me = lax.axis_index("lat")
    tm_first = lax.axis_index("tm") == 0
    most = jnp.max(jnp.max(jnp.abs(second[...]), axis=0), axis=0, keepdims=True)
    most = jnp.maximum(jnp.max(most, axis=1, keepdims=True), 1e-30)
    inverse = jnp.broadcast_to(1.0 / most, (1, first.shape[2]))
    sums = [jnp.zeros((1, first.shape[2]), F32) for _ in range(4)]
    for shift, block in enumerate((p0, p1, p2, p3)):
        at = me ^ shift
        r0, v1 = first[at], second[at]
        misfit, weight = next_misfit(at, shift, later, z, precision)
        initial = jnp.where(tm_first, block[...].astype(F32), 0.0)
        near, far = v1 * inverse, misfit * inverse
        square = near * near
        terms = (r0 * r0, r0 * v1, square, weight * far * far + initial * square)
        sums = [total + jnp.sum(term, axis=0, keepdims=True) for total, term in zip(sums, terms)]
    reach = energy[:BANDS, :] * inverse[:, :TILE]
    observed = jnp.sum(reach * reach * energy[BANDS:, :], axis=0, keepdims=True)
    for j, total in enumerate(sums):
        value = jnp.broadcast_to(jnp.sum(total, axis=1, keepdims=True), (1, TILE))
        dots[j : j + 1, :] = value + observed if j == 3 else value
    dots[4:5, :] = jnp.broadcast_to(most, (1, TILE))
    dots[5:8, :] = jnp.zeros((3, TILE), F32)


def finish_kernel(d0, d1, d2, d3, first, second, earlier, adjoint, p0, inc, res):
    me = lax.axis_index("lat")
    chan, _, lon = inc.shape
    shares = [d[...] for d in (d0, d1, d2, d3)]
    mosts = [share[4:5, :1] for share in shares]
    most = jnp.maximum(jnp.maximum(mosts[0], mosts[1]), jnp.maximum(mosts[2], mosts[3]))
    added = lambda values: (values[0] + values[1]) + (values[2] + values[3])
    rr0 = added([share[0:1, :1] for share in shares])
    c0 = added([share[1:2, :1] for share in shares]) / SHRINK
    g11, g12 = [
        added([share[j : j + 1, :1] * (own / most) * (own / most) for share, own in zip(shares, mosts)])
        for j in (2, 3)
    ]
    a0 = rr0 / c0
    full = most / SHRINK
    reach = a0 * full
    rr1 = rr0 - 2.0 * a0 * c0 + reach * reach * g11
    beta = rr1 / rr0
    grow = 1.0 + beta
    c1 = grow * grow * c0 - 2.0 * grow * reach * full * g11 + reach * reach * g12
    a1 = rr1 / c1
    wide = lambda value: jnp.broadcast_to(value, (chan, lon))
    step, cross = wide(a0 + a1 * grow), wide(a1 * a0 / SHRINK)
    along = step / SHRINK
    image = image_of(me, p0[...], second, earlier, adjoint)
    r0_own, v1_own = first[me], second[me]
    for row in range(2):
        at = row * CHAN
        r0, v1, v2 = [field[at : at + chan] for field in (r0_own, v1_own, image)]
        inc[:, row, :] = step * r0 - cross * v1
        res[:, row, :] = r0 - along * v1 + cross * v2


VMEM = pl.BlockSpec(memory_space=pltpu.VMEM)
SMEM = pl.BlockSpec(memory_space=pltpu.SMEM)


def call(kernel, name, ins, outs, scratch=(), scalars=0):
    specs = [SMEM] * scalars + [VMEM] * (len(ins) - scalars)
    return pl.pallas_call(
        kernel,
        name=name,
        out_shape=outs,
        in_specs=specs,
        out_specs=[VMEM] * len(outs),
        scratch_shapes=list(scratch),
        compiler_params=pltpu.CompilerParams(vmem_limit_bytes=48 << 20),
        cost_estimate=pl.CostEstimate(flops=1, bytes_accessed=1, transcendentals=0),
    )(*ins)


def stack_in(kernel):
    rows, cols, out_c, in_c = kernel.shape
    padded = jnp.pad(kernel, ((0, 0), (0, 0), (0, 0), (0, CHAN_IN - in_c)))
    block = jnp.transpose(padded, (2, 0, 1, 3)).reshape(out_c, rows, cols * CHAN_IN)
    block = jnp.pad(block, ((0, 0), (0, 0), (0, TAPS - cols * CHAN_IN)))
    return block.reshape(out_c, rows * TAPS)


def stack_out(kernel):
    rows, cols, out_c, in_c = kernel.shape
    padded = jnp.pad(kernel, ((0, 0), (0, 0), (0, CHAN - out_c), (0, 0)))
    none = jnp.zeros_like(padded[0])
    tap = lambda row_off: padded[row_off] if 0 <= row_off < rows else none
    blocks = [jnp.concatenate([tap(t - m) for t in range(4)], axis=-1) for m in range(2)]
    return jnp.concatenate(blocks, axis=0).reshape(2 * cols * CHAN, 4 * in_c)


def as_band(cells):
    rows, chan, lon = cells.shape
    return jnp.pad(cells.astype(BF16), ((0, 0), (0, CHAN - chan), (0, 0))).reshape(PAIR, lon)


def swap(block, shift):
    count = lax.axis_size("lat")
    return lax.ppermute(block, "lat", [(i, i ^ shift) for i in range(count)])


def by_partner(value):
    far = swap(value, 2)
    return [value, swap(value, 1), far, swap(far, 1)]


def along_tm(value, step):
    count = lax.axis_size("tm")
    return lax.ppermute(value, "tm", [(i, (i + step) % count) for i in range(count)])


def row_plan(
    departures,
    error_precision,
    trajectory,
    conv_in,
    conv_out,
    hidden_bias,
    step_counts,
    obs_tiles,
    obs_weights,
    innovations,
    obs_precision,
):
    _, rows, chan, lon = departures.shape
    hid = conv_in.shape[2]
    shape = lambda *dims: jax.ShapeDtypeStruct(dims, F32)
    shape_b = lambda *dims: jax.ShapeDtypeStruct(dims, BF16)
    whole, whole_b = shape(BANDS, PAIR, lon), shape_b(BANDS, PAIR, lon)

    root = jnp.sqrt(obs_precision[0])
    tiles = obs_tiles[0]
    per_row = 2 * chan
    slot = (2 * (tiles // per_row) + tiles % 2) * CHAN + (tiles // 2) % chan
    innov_high, innov_low = split_16(root * innovations[0])
    table = lambda value: value.astype(BF16).reshape(1, 2 * TILE)
    weights = (obs_weights[0] * root[:, None]).astype(BF16)
    obs_own = jnp.concatenate(
        [
            jnp.concatenate([weights[:TILE], weights[TILE:]], axis=1),
            table(slot // 2),
            table(slot % 2),
            table(innov_high),
            table(innov_low),
            jnp.zeros((OBS_ROWS - TILE - 4, 2 * TILE), BF16),
        ],
        axis=0,
    )
    both_own = jnp.stack([as_band(trajectory[0]), obs_own])
    prec_own = as_band(error_precision[0])

    y_own = as_band(error_precision[0] * departures[0])
    y_all = [y_own, swap(y_own, 1), swap(y_own, 2), swap(y_own, 3)]
    b_all = by_partner(both_own)
    p_all = by_partner(prec_own)
    y_later = along_tm(jnp.stack(y_all), -1)
    p_later = along_tm(jnp.stack(p_all), -1)

    fore_in, fore_out = stack_in(conv_in), stack_out(conv_out)
    back_in, back_out = stack_in(flipped(conv_out)), stack_out(flipped(conv_in))
    taps = pltpu.VMEM((ROWS, TAPS, lon), BF16)
    hidden = pltpu.VMEM((ROWS + 2, hid, lon), BF16)
    field = pltpu.VMEM((BANDS, PAIR, lon), F32)

    gate_shape = shape_b(ROWS, hid, lon)
    gate, r0, r0_b = call(
        rhs_kernel,
        "rhs",
        (step_counts, *y_all, y_later, *b_all, fore_in, hidden_bias[:, None], back_in, back_out),
        [gate_shape, whole, whole_b],
        [field, taps, hidden],
        1,
    )
    later = along_tm(r0_b, -1)
    z1, z1_b = call(
        forward_kernel,
        "forward",
        (step_counts, r0, gate, fore_in, fore_out),
        [whole, whole_b],
        [taps, hidden],
        1,
    )
    earlier = along_tm(z1_b, 1)
    observed, pick, spread, weights = call(
        observe_kernel,
        "observe",
        (z1, *b_all),
        [
            whole,
            shape_b(BANDS, 2 * TILE, SLOTS),
            shape_b(BANDS, SLOTS, 2 * TILE),
            shape(BANDS, 2 * TILE, TILE),
        ],
    )
    (adjoint,) = call(
        adjoint_kernel,
        "adjoint",
        (step_counts, observed, z1, later, p_later, gate, back_in, back_out),
        [whole],
        [taps, hidden],
        1,
    )
    v1, v1_b = call(image_kernel, "image", (r0, earlier, adjoint, *p_all), [whole, whole_b])
    later = along_tm(v1_b, -1)
    z2, z2_b = call(
        forward_kernel,
        "forward",
        (step_counts, v1, gate, fore_in, fore_out),
        [whole, whole_b],
        [taps, hidden],
        1,
    )
    earlier = along_tm(z2_b, 1)
    observed, energy = call(
        observe_again_kernel,
        "observe_again",
        (z2, pick, spread, weights),
        [whole, shape(8, TILE)],
    )
    (dots,) = call(
        products_kernel,
        "products",
        (r0, v1, z2, later, p_later, *p_all, energy),
        [shape(8, TILE)],
    )
    count = lax.axis_size("tm")
    parts = [dots] + [
        lax.ppermute(dots, "tm", [(i, i ^ step) for i in range(count)]) for step in range(1, count)
    ]
    observed, _ = lax.optimization_barrier((observed, dots))
    (adjoint,) = call(
        adjoint_kernel,
        "adjoint",
        (step_counts, observed, z2, later, p_later, gate, back_in, back_out),
        [whole],
        [taps, hidden],
        1,
    )
    inc, res = call(
        finish_kernel,
        "finish",
        (*parts, r0, v1, earlier, adjoint, p_all[0]),
        [shape(chan, rows, lon)] * 2,
    )
    return (jnp.transpose(inc, (1, 0, 2))[None], jnp.transpose(res, (1, 0, 2))[None])


def solution(mesh):
    in_specs = (
        P(("ens", "tm"), "lat", None, None),
        P(("ens", "tm"), "lat", None, None),
        P(("ens", "tm"), "lat", None, None),
        P(),
        P(),
        P(),
        P(("ens", "tm")),
        P(("ens", "tm"), "lat"),
        P(("ens", "tm"), "lat", None),
        P(("ens", "tm"), "lat"),
        P(("ens", "tm"), "lat"),
    )
    out_specs = (P(("ens", "tm"), "lat", None, None), P(("ens", "tm"), "lat", None, None))
    plan = row_plan if mesh.shape["lat"] == BANDS and mesh.shape["tm"] == 4 else halo_plan
    return jax.shard_map(plan, mesh=mesh, in_specs=in_specs, out_specs=out_specs, check_vma=False)
```

```python
import functools

import jax
import jax.numpy as jnp
from jax import lax
from jax.experimental import pallas as pl
from jax.experimental.pallas import tpu as pltpu
from jax.sharding import PartitionSpec as P

TILE = 128
STEPS = 2
ITERS = 2
F32 = jnp.float32
BF16 = jnp.bfloat16


def padded_2(cells, sides, width):
    for axis, dim in sides:
        count = lax.axis_size(axis)
        ends = count - 1
        head = lax.slice_in_dim(cells, 0, width, axis=dim)
        tail = lax.slice_in_dim(cells, cells.shape[dim] - width, cells.shape[dim], axis=dim)
        cells = jnp.concatenate(
            [
                lax.ppermute(tail, axis, [(i, (i + 1) % count) for i in range(ends)]),
                cells,
                lax.ppermute(head, axis, [((i + 1) % count, i) for i in range(ends)]),
            ],
            axis=dim,
        )
    return cells


def from_behind(value, axis, steps):
    count = lax.axis_size(axis)
    leading, last = (max(0, -steps), min(count, count - steps))
    return lax.ppermute(value, axis, [(source, source + steps) for source in range(leading, last)])


def convolve_padded(padded, kernel):
    out_rows = padded.shape[0] - 2
    lon_len = padded.shape[2]
    wrapped = jnp.concatenate([padded[:, :, -1:], padded, padded[:, :, :1]], axis=2)
    accumulated = None
    for row_off in range(3):
        for col_off in range(3):
            window = wrapped[row_off : row_off + out_rows, :, col_off : col_off + lon_len]
            term = jnp.einsum(
                "oi,ril->rol", kernel[row_off, col_off], window, preferred_element_type=F32
            )
            accumulated = term if accumulated is None else accumulated + term
    return accumulated


def flipped(kernel):
    return jnp.transpose(kernel[::-1, ::-1], (0, 1, 3, 2))


def rim_wide(source):
    return padded_2(source, (("lat", 0),), 2)


def shift_up(source):
    return from_behind(source.astype(BF16), "tm", -1).astype(source.dtype)


def global_squares(source):
    return lax.psum(jnp.sum(source * source), ("tm", "lat"))


def halo_plan(
    departures,
    error_precision,
    trajectory,
    conv_in,
    conv_out,
    hidden_bias,
    step_counts,
    obs_tiles,
    obs_weights,
    innovations,
    obs_precision,
):
    precision = error_precision[0]
    own_count = step_counts[0]
    tile_index = obs_tiles[0]
    weights = obs_weights[0]
    innovation = innovations[0]
    obs_scale = obs_precision[0]
    back_in = flipped(conv_in)
    back_out = flipped(conv_out)
    trajectory_ext = padded_2(trajectory[0], (("lat", 0),), 1)
    gate_factor = (
        1.0 - jnp.tanh(convolve_padded(trajectory_ext, conv_in) + hidden_bias[:, None]) ** 2
    ).astype(BF16)
    gate_wide = padded_2(gate_factor, (("lat", 0),), 1)

    def one_step(current, first_kernel, second_kernel):
        widened = rim_wide(current.astype(BF16))
        hidden = (gate_wide.astype(F32) * convolve_padded(widened, first_kernel)).astype(BF16)
        return current + convolve_padded(hidden, second_kernel)

    def model(current, first_kernel, second_kernel):
        for step_index in range(STEPS):
            current = jnp.where(
                step_index < own_count, one_step(current, first_kernel, second_kernel), current
            )
        return current

    def observe_adjoint(scaled, like):
        tile_table = (
            jnp.zeros((like.size // TILE, TILE), F32)
            .at[tile_index]
            .add(weights * scaled[:, None])
        )
        return tile_table.reshape(like.shape)

    first_weighted = precision * departures[0]
    rhs = first_weighted + model(
        observe_adjoint(obs_scale * innovation, first_weighted) - shift_up(first_weighted),
        back_out,
        back_in,
    )
    increment = jnp.zeros_like(rhs)
    residual = rhs
    direction = rhs
    norm_now = global_squares(residual)
    for _ in range(ITERS):
        propagated = model(direction, conv_in, conv_out)
        earlier = from_behind(propagated.astype(BF16), "tm", 1).astype(F32)
        weighted = precision * (direction - earlier)
        picked = propagated.reshape(-1, TILE)[tile_index]
        observed = jnp.sum(picked * weights, axis=1)
        operator_image = weighted + model(
            observe_adjoint(obs_scale * observed, direction) - shift_up(weighted),
            back_out,
            back_in,
        )
        curvature = lax.psum(jnp.sum(direction * operator_image), ("tm", "lat"))
        step_length = norm_now / curvature
        increment = increment + step_length * direction
        residual = residual - step_length * operator_image
        norm_next = global_squares(residual)
        direction = residual + norm_next / norm_now * direction
        norm_now = norm_next
    return (increment[None], residual[None])


BANDS = 4
ROWS = 2 * BANDS
CHAN = 72
CHAN_IN = 80
TAPS = 256
PAIR = 2 * CHAN
SLOTS = 4 * CHAN
OBS_ROWS = 144
SHRINK = 2.0**-16


def row_of(ref, row):
    return ref[row // 2, (row % 2) * CHAN : (row % 2 + 1) * CHAN, :]


def taps_of(row):
    zeros = jnp.zeros((CHAN_IN - CHAN, row.shape[1]), F32)
    right = pltpu.roll(row, 1, axis=1)
    left = pltpu.roll(row, row.shape[1] - 1, axis=1)
    return jnp.concatenate([right, zeros, row, zeros, left, zeros], axis=0).astype(BF16)


def clear_taps(taps):
    used = 3 * CHAN_IN
    taps[:, used:, :] = jnp.zeros((ROWS, TAPS - used, taps.shape[2]), BF16)


def conv_rows(field, w_in, taps, emit):
    for row in range(ROWS):
        taps[row, : 3 * CHAN_IN] = taps_of(row_of(field, row))
    for row in range(ROWS):
        low, high = max(row - 1, 0), min(row + 2, ROWS)
        stacked = taps[low:high].reshape((high - low) * TAPS, taps.shape[2])
        skip = (low - (row - 1)) * TAPS
        weights = w_in[:, skip : skip + (high - low) * TAPS]
        emit(row, jnp.dot(weights, stacked, preferred_element_type=F32))


def prepare(taps, hidden):
    clear_taps(taps)
    hidden[0] = jnp.zeros(hidden.shape[1:], BF16)
    hidden[ROWS + 1] = jnp.zeros(hidden.shape[1:], BF16)


def model_step(source, target, target_b, gate, w_in, w_out, taps, hidden):
    def gated(row, value):
        hidden[row + 1] = (gate[row].astype(F32) * value).astype(BF16)

    conv_rows(source, w_in, taps, gated)
    for pair in range(BANDS):
        stacked = hidden[2 * pair : 2 * pair + 4].reshape(-1, hidden.shape[2])
        part = jnp.dot(w_out[...], stacked, preferred_element_type=F32)
        lon = part.shape[1]
        rows = []
        for row in range(2):
            tap = [part[(3 * row + b) * CHAN : (3 * row + b + 1) * CHAN] for b in range(3)]
            spread = pltpu.roll(tap[0], 1, axis=1) + tap[1] + pltpu.roll(tap[2], lon - 1, axis=1)
            rows.append(source[pair, row * CHAN : (row + 1) * CHAN, :] + spread)
        band = jnp.concatenate(rows, axis=0)
        target[pair] = band
        if target_b is not None:
            target_b[pair] = band.astype(BF16)


def model_steps(field, gate, w_in, w_out, taps, hidden, count):
    prepare(taps, hidden)

    def one_step(_, carry):
        model_step(field, field, None, gate, w_in, w_out, taps, hidden)
        return carry

    lax.fori_loop(0, jnp.minimum(count, STEPS), one_step, 0)


def forward_steps(start, out, out_b, gate, w_in, w_out, taps, hidden, count):
    prepare(taps, hidden)
    model_step(start, out, out_b, gate, w_in, w_out, taps, hidden)

    def one_step(_, carry):
        model_step(out, out, out_b, gate, w_in, w_out, taps, hidden)
        return carry

    lax.fori_loop(1, jnp.minimum(count, STEPS), one_step, 0)


def split_16(value):
    high = value.astype(BF16)
    low = (value - high.astype(F32)).astype(BF16)
    return high, low


def obs_of(obs):
    weights = jnp.concatenate([obs[:TILE, :TILE], obs[:TILE, TILE:]], axis=0)
    extra = obs[TILE:, :].astype(F32)
    return weights, 2.0 * extra[0:1] + extra[1:2], extra[2:3], extra[3:4]


def one_hot_t(slot):
    iota = lax.broadcasted_iota(jnp.int32, (SLOTS, 2 * TILE), 0).astype(F32)
    return (iota == slot).astype(F32)


def one_hot(slot):
    columns = [
        jnp.transpose(jnp.broadcast_to(slot[:, half * TILE : (half + 1) * TILE], (TILE, TILE)))[:, :1]
        for half in range(2)
    ]
    column = jnp.concatenate(columns, axis=0)
    iota = lax.broadcasted_iota(jnp.int32, (2 * TILE, SLOTS), 1).astype(F32)
    return (iota == column).astype(F32)


def band_slots(band):
    return jnp.concatenate(
        [
            band[row * CHAN : (row + 1) * CHAN, half * TILE : (half + 1) * TILE]
            for row in range(2)
            for half in range(2)
        ],
        axis=0,
    )


def slots_band(slots):
    return jnp.concatenate(
        [
            jnp.concatenate(
                [slots[(2 * row + half) * CHAN : (2 * row + half + 1) * CHAN] for half in range(2)],
                axis=1,
            )
            for row in range(2)
        ],
        axis=0,
    )


def rhs_kernel(
    counts,
    y0, y1, y2, y3,
    later,
    b0, b1, b2, b3,
    fore_in, bias, w_in, w_out,
    gate, out, out_b,
    field, taps, hidden,
):
    me = lax.axis_index("lat")
    more = lax.axis_index("tm") < lax.axis_size("tm") - 1
    blocks = (b0, b1, b2, b3)
    for shift, block in enumerate(blocks):
        field[me ^ shift] = block[0].astype(F32)
    prepare(taps, hidden)

    def emit(row, value):
        squashed = jnp.tanh(value + bias[...])
        gate[row] = (1.0 - squashed * squashed).astype(BF16)

    conv_rows(field, fore_in, taps, emit)
    for shift, block in enumerate(blocks):
        weights, slot, high, low = obs_of(block[1])
        hot = one_hot_t(slot)
        both = jnp.concatenate([hot * high, hot * low], axis=1).astype(BF16)
        slots = jnp.dot(
            both, jnp.concatenate([weights, weights], axis=0), preferred_element_type=F32
        )
        next_y = jnp.where(more, later[shift].astype(F32), 0.0)
        field[me ^ shift] = slots_band(slots) - next_y

    def one_step(_, carry):
        model_step(field, field, None, gate, w_in, w_out, taps, hidden)
        return carry

    lax.fori_loop(0, jnp.minimum(counts[0], STEPS), one_step, 0)
    for shift, block in enumerate((y0, y1, y2, y3)):
        total = field[me ^ shift] + block[...].astype(F32)
        out[me ^ shift] = total
        out_b[me ^ shift] = total.astype(BF16)


def forward_kernel(counts, start, gate, w_in, w_out, out, out_b, taps, hidden):
    forward_steps(start, out, out_b, gate, w_in, w_out, taps, hidden, counts[0])


def observed_band(z_band, pick, spread, weights):
    ones = jnp.ones((2 * TILE, TILE), BF16)

    def product(left, value):
        return jnp.dot(left, jnp.concatenate(split_16(value), axis=1), preferred_element_type=F32)

    picked = product(pick, band_slots(z_band))
    terms = (picked[:, :TILE] + picked[:, TILE:]) * weights
    terms = jnp.concatenate(split_16(terms), axis=1)
    scaled = jnp.dot(terms, ones, preferred_element_type=F32)
    slots = product(spread, weights * scaled)
    most = jnp.maximum(jnp.max(jnp.abs(scaled), axis=0, keepdims=True), 1e-30)
    near = scaled * (1.0 / most)
    squares = jnp.sum(near * near, axis=0, keepdims=True)
    return slots_band(slots[:, :TILE] + slots[:, TILE:]), most, squares


def observe_kernel(z, b0, b1, b2, b3, out, pick, spread, weights):
    me = lax.axis_index("lat")
    for shift, block in enumerate((b0, b1, b2, b3)):
        at = me ^ shift
        own, slot, _, _ = obs_of(block[1])
        pick[at] = one_hot(slot).astype(BF16)
        spread[at] = one_hot_t(slot).astype(BF16)
        weights[at] = own.astype(F32)
    for band in range(BANDS):
        out[band], _, _ = observed_band(z[band], pick[band], spread[band], weights[band])


def observe_again_kernel(z, pick, spread, weights, out, energy):
    for band in range(BANDS):
        out[band], most, squares = observed_band(z[band], pick[band], spread[band], weights[band])
        energy[band : band + 1, :] = most
        energy[BANDS + band : BANDS + band + 1, :] = squares


def next_misfit(at, shift, later, z, precision):
    more = lax.axis_index("tm") < lax.axis_size("tm") - 1
    weight = jnp.where(more, precision[shift].astype(F32), 0.0)
    return later[at].astype(F32) - z[at], weight


def adjoint_kernel(
    counts, observed, z, later, precision, gate, w_in, w_out, field, taps, hidden
):
    me = lax.axis_index("lat")
    for shift in range(BANDS):
        at = me ^ shift
        misfit, weight = next_misfit(at, shift, later, z, precision)
        field[at] = observed[at] - weight * misfit
    model_steps(field, gate, w_in, w_out, taps, hidden, counts[0])


def image_of(at, block, start, earlier, adjoint):
    before = jnp.where(lax.axis_index("tm") == 0, 0.0, earlier[at].astype(F32))
    return block.astype(F32) * (start[at] - before) + adjoint[at]


def image_kernel(start, earlier, adjoint, p0, p1, p2, p3, out, out_b):
    me = lax.axis_index("lat")
    for shift, block in enumerate((p0, p1, p2, p3)):
        at = me ^ shift
        total = SHRINK * image_of(at, block[...], start, earlier, adjoint)
        out[at] = total
        out_b[at] = total.astype(BF16)


def products_kernel(first, second, z, later, precision, p0, p1, p2, p3, energy, dots):
    me = lax.axis_index("lat")
    tm_first = lax.axis_index("tm") == 0
    most = jnp.max(jnp.max(jnp.abs(second[...]), axis=0), axis=0, keepdims=True)
    most = jnp.maximum(jnp.max(most, axis=1, keepdims=True), 1e-30)
    inverse = jnp.broadcast_to(1.0 / most, (1, first.shape[2]))
    sums = [jnp.zeros((1, first.shape[2]), F32) for _ in range(4)]
    for shift, block in enumerate((p0, p1, p2, p3)):
        at = me ^ shift
        r0, v1 = first[at], second[at]
        misfit, weight = next_misfit(at, shift, later, z, precision)
        initial = jnp.where(tm_first, block[...].astype(F32), 0.0)
        near, far = v1 * inverse, misfit * inverse
        square = near * near
        terms = (r0 * r0, r0 * v1, square, weight * far * far + initial * square)
        sums = [total + jnp.sum(term, axis=0, keepdims=True) for total, term in zip(sums, terms)]
    reach = energy[:BANDS, :] * inverse[:, :TILE]
    observed = jnp.sum(reach * reach * energy[BANDS:, :], axis=0, keepdims=True)
    for j, total in enumerate(sums):
        value = jnp.broadcast_to(jnp.sum(total, axis=1, keepdims=True), (1, TILE))
        dots[j : j + 1, :] = value + observed if j == 3 else value
    dots[4:5, :] = jnp.broadcast_to(most, (1, TILE))
    dots[5:8, :] = jnp.zeros((3, TILE), F32)


def finish_kernel(d0, d1, d2, d3, first, second, earlier, adjoint, p0, inc, res):
    me = lax.axis_index("lat")
    chan, _, lon = inc.shape
    shares = [d[...] for d in (d0, d1, d2, d3)]
    mosts = [share[4:5, :1] for share in shares]
    most = jnp.maximum(jnp.maximum(mosts[0], mosts[1]), jnp.maximum(mosts[2], mosts[3]))
    added = lambda values: (values[0] + values[1]) + (values[2] + values[3])
    rr0 = added([share[0:1, :1] for share in shares])
    c0 = added([share[1:2, :1] for share in shares]) / SHRINK
    g11, g12 = [
        added([share[j : j + 1, :1] * (own / most) * (own / most) for share, own in zip(shares, mosts)])
        for j in (2, 3)
    ]
    a0 = rr0 / c0
    full = most / SHRINK
    reach = a0 * full
    rr1 = rr0 - 2.0 * a0 * c0 + reach * reach * g11
    beta = rr1 / rr0
    grow = 1.0 + beta
    c1 = grow * grow * c0 - 2.0 * grow * reach * full * g11 + reach * reach * g12
    a1 = rr1 / c1
    wide = lambda value: jnp.broadcast_to(value, (chan, lon))
    step, cross = wide(a0 + a1 * grow), wide(a1 * a0 / SHRINK)
    along = step / SHRINK
    image = image_of(me, p0[...], second, earlier, adjoint)
    r0_own, v1_own = first[me], second[me]
    for row in range(2):
        at = row * CHAN
        r0, v1, v2 = [field[at : at + chan] for field in (r0_own, v1_own, image)]
        inc[:, row, :] = step * r0 - cross * v1
        res[:, row, :] = r0 - along * v1 + cross * v2


VMEM = pl.BlockSpec(memory_space=pltpu.VMEM)
SMEM = pl.BlockSpec(memory_space=pltpu.SMEM)


def call(kernel, name, ins, outs, scratch=(), scalars=0):
    specs = [SMEM] * scalars + [VMEM] * (len(ins) - scalars)
    return pl.pallas_call(
        kernel,
        name=name,
        out_shape=outs,
        in_specs=specs,
        out_specs=[VMEM] * len(outs),
        scratch_shapes=list(scratch),
        compiler_params=pltpu.CompilerParams(vmem_limit_bytes=48 << 20),
        cost_estimate=pl.CostEstimate(flops=2 * 10**9, bytes_accessed=1, transcendentals=0),
    )(*ins)


def stack_in(kernel):
    rows, cols, out_c, in_c = kernel.shape
    padded = jnp.pad(kernel, ((0, 0), (0, 0), (0, 0), (0, CHAN_IN - in_c)))
    block = jnp.transpose(padded, (2, 0, 1, 3)).reshape(out_c, rows, cols * CHAN_IN)
    block = jnp.pad(block, ((0, 0), (0, 0), (0, TAPS - cols * CHAN_IN)))
    return block.reshape(out_c, rows * TAPS)


def stack_out(kernel):
    rows, cols, out_c, in_c = kernel.shape
    padded = jnp.pad(kernel, ((0, 0), (0, 0), (0, CHAN - out_c), (0, 0)))
    none = jnp.zeros_like(padded[0])
    tap = lambda row_off: padded[row_off] if 0 <= row_off < rows else none
    blocks = [jnp.concatenate([tap(t - m) for t in range(4)], axis=-1) for m in range(2)]
    return jnp.concatenate(blocks, axis=0).reshape(2 * cols * CHAN, 4 * in_c)


def as_band(cells):
    rows, chan, lon = cells.shape
    return jnp.pad(cells.astype(BF16), ((0, 0), (0, CHAN - chan), (0, 0))).reshape(PAIR, lon)


def swap(block, shift):
    count = lax.axis_size("lat")
    return lax.ppermute(block, "lat", [(i, i ^ shift) for i in range(count)])


def by_partner(value):
    far = swap(value, 2)
    return [value, swap(value, 1), far, swap(far, 1)]


def along_tm(value, step):
    count = lax.axis_size("tm")
    return lax.ppermute(value, "tm", [(i, (i + step) % count) for i in range(count)])


def row_plan(
    departures,
    error_precision,
    trajectory,
    conv_in,
    conv_out,
    hidden_bias,
    step_counts,
    obs_tiles,
    obs_weights,
    innovations,
    obs_precision,
):
    _, rows, chan, lon = departures.shape
    hid = conv_in.shape[2]
    shape = lambda *dims: jax.ShapeDtypeStruct(dims, F32)
    shape_b = lambda *dims: jax.ShapeDtypeStruct(dims, BF16)
    whole, whole_b = shape(BANDS, PAIR, lon), shape_b(BANDS, PAIR, lon)

    root = jnp.sqrt(obs_precision[0])
    tiles = obs_tiles[0]
    per_row = 2 * chan
    slot = (2 * (tiles // per_row) + tiles % 2) * CHAN + (tiles // 2) % chan
    innov_high, innov_low = split_16(root * innovations[0])
    table = lambda value: value.astype(BF16).reshape(1, 2 * TILE)
    weights = (obs_weights[0] * root[:, None]).astype(BF16)
    obs_own = jnp.concatenate(
        [
            jnp.concatenate([weights[:TILE], weights[TILE:]], axis=1),
            table(slot // 2),
            table(slot % 2),
            table(innov_high),
            table(innov_low),
            jnp.zeros((OBS_ROWS - TILE - 4, 2 * TILE), BF16),
        ],
        axis=0,
    )
    both_own = jnp.stack([as_band(trajectory[0]), obs_own])
    prec_own = as_band(error_precision[0])

    y_own = as_band(error_precision[0] * departures[0])
    y_all = [y_own, swap(y_own, 1), swap(y_own, 2), swap(y_own, 3)]
    b_all = by_partner(both_own)
    p_all = by_partner(prec_own)
    y_later = along_tm(jnp.stack(y_all), -1)
    p_later = along_tm(jnp.stack(p_all), -1)

    fore_in, fore_out = stack_in(conv_in), stack_out(conv_out)
    back_in, back_out = stack_in(flipped(conv_out)), stack_out(flipped(conv_in))
    taps = pltpu.VMEM((ROWS, TAPS, lon), BF16)
    hidden = pltpu.VMEM((ROWS + 2, hid, lon), BF16)
    field = pltpu.VMEM((BANDS, PAIR, lon), F32)

    gate_shape = shape_b(ROWS, hid, lon)
    gate, r0, r0_b = call(
        rhs_kernel,
        "rhs",
        (step_counts, *y_all, y_later, *b_all, fore_in, hidden_bias[:, None], back_in, back_out),
        [gate_shape, whole, whole_b],
        [field, taps, hidden],
        1,
    )
    later = along_tm(r0_b, -1)
    z1, z1_b = call(
        forward_kernel,
        "forward",
        (step_counts, r0, gate, fore_in, fore_out),
        [whole, whole_b],
        [taps, hidden],
        1,
    )
    earlier = along_tm(z1_b, 1)
    observed, pick, spread, weights = call(
        observe_kernel,
        "observe",
        (z1, *b_all),
        [
            whole,
            shape_b(BANDS, 2 * TILE, SLOTS),
            shape_b(BANDS, SLOTS, 2 * TILE),
            shape(BANDS, 2 * TILE, TILE),
        ],
    )
    (adjoint,) = call(
        adjoint_kernel,
        "adjoint",
        (step_counts, observed, z1, later, p_later, gate, back_in, back_out),
        [whole],
        [taps, hidden],
        1,
    )
    v1, v1_b = call(image_kernel, "image", (r0, earlier, adjoint, *p_all), [whole, whole_b])
    later = along_tm(v1_b, -1)
    z2, z2_b = call(
        forward_kernel,
        "forward",
        (step_counts, v1, gate, fore_in, fore_out),
        [whole, whole_b],
        [taps, hidden],
        1,
    )
    earlier = along_tm(z2_b, 1)
    observed, energy = call(
        observe_again_kernel,
        "observe_again",
        (z2, pick, spread, weights),
        [whole, shape(8, TILE)],
    )
    (dots,) = call(
        products_kernel,
        "products",
        (r0, v1, z2, later, p_later, *p_all, energy),
        [shape(8, TILE)],
    )
    count = lax.axis_size("tm")
    parts = [dots] + [
        lax.ppermute(dots, "tm", [(i, i ^ step) for i in range(count)]) for step in range(1, count)
    ]
    observed, _ = lax.optimization_barrier((observed, dots))
    (adjoint,) = call(
        adjoint_kernel,
        "adjoint",
        (step_counts, observed, z2, later, p_later, gate, back_in, back_out),
        [whole],
        [taps, hidden],
        1,
    )
    inc, res = call(
        finish_kernel,
        "finish",
        (*parts, r0, v1, earlier, adjoint, p_all[0]),
        [shape(chan, rows, lon)] * 2,
    )
    return (jnp.transpose(inc, (1, 0, 2))[None], jnp.transpose(res, (1, 0, 2))[None])


def solution(mesh):
    in_specs = (
        P(("ens", "tm"), "lat", None, None),
        P(("ens", "tm"), "lat", None, None),
        P(("ens", "tm"), "lat", None, None),
        P(),
        P(),
        P(),
        P(("ens", "tm")),
        P(("ens", "tm"), "lat"),
        P(("ens", "tm"), "lat", None),
        P(("ens", "tm"), "lat"),
        P(("ens", "tm"), "lat"),
    )
    out_specs = (P(("ens", "tm"), "lat", None, None), P(("ens", "tm"), "lat", None, None))
    plan = row_plan if mesh.shape["lat"] == BANDS and mesh.shape["tm"] == 4 else halo_plan
    return jax.shard_map(plan, mesh=mesh, in_specs=in_specs, out_specs=out_specs, check_vma=False)
```
